32 devices in a mesh: ens: 2 (over x), lon: 4 (over y, core), lat: 4 (over z).
Axes of the slice: x: 2, y: 2, z: 4, core: 2. Of those that a mesh axis runs over, the one named last changes fastest.
Arguments:
- members: float32 [2, 80, 32, 640], P('ens', 'lat', 'lon'), may hold values from -6 to 6
- analysis: float32 [80, 32, 640], P('lat', 'lon', 'ens'), may hold values from -6 to 6
- stencils: float32 [7, 7, 7, 80], replicated, may hold values from -0.84 to 0.84
- mixing: float32 [7, 640, 640], replicated, may hold values from -0.09375 to 0.09375
Outputs:
- members_grad: float32 [2, 80, 32, 640], P('ens', 'lat', 'lon')
- crps_field: float32 [80, 32, 640], P('lat', 'lon', 'ens')
The draws below stay inside these ranges and needn't reach their ends.
All inputs are finite; a program needn't handle non-finite values.
Results may differ from the reference program's by a relative error of at most 0.00016.
Values sent between devices are 32-bit elements; how exact they have to be, the bound alone decides.
No kernel may reach another device: no remote copies, remote signals or barrier semaphores. Data moves between devices by JAX's collectives and lax.ppermute only.
A program may use at most 128 MiB of HBM per device.

```python
import jax
import jax.numpy as jnp
from jax import lax

C = 640
BASES = 7
SPAN = 7
MEMBERS = 2
LAT_ROWS = 80
LON_COLS = 32


def level_of(stream_key, shape, pieces, least, top_value):
    def one(dim, shards_of):
        heights = jax.random.uniform(jax.random.fold_in(jax.random.fold_in(stream_key, 6), dim), (shards_of,), jnp.float32, least / len(pieces), top_value / len(pieces))
        return jnp.repeat(jnp.exp(heights), shape[dim] // shards_of).reshape((-1,) + (1,) * (len(shape) - dim - 1))

    level = one(*pieces[0])
    for cut in pieces[1:]:
        level = level * one(*cut)
    return level


def centred(key, dims, width, most, cuts=(), held_as=jnp.bfloat16):
    gain = level_of(key, dims, cuts, -0.22, 0.18) if cuts else 1.0
    entries = jax.random.normal(key, dims, jnp.float32) * width * gain
    return jnp.minimum(jnp.maximum(entries, -most), most).astype(held_as)


def setup_inputs(seed: int = 0) -> dict:
    streams_of = jax.random.split(jax.random.key(seed), 5)
    members = centred(streams_of[0], (MEMBERS, LAT_ROWS, LON_COLS, C), 1.0, 6.0, ((0, 2), (1, 4), (2, 4)), jnp.float32)
    analysis = centred(streams_of[1], (LAT_ROWS, LON_COLS, C), 1.0, 6.0, ((0, 4), (1, 4), (2, 2)), jnp.float32)
    stencils = centred(streams_of[2], (BASES, SPAN, SPAN, LAT_ROWS), 0.14, 0.84, (), jnp.float32)
    mixing = centred(streams_of[3], (BASES, C, C), (BASES * C) ** -0.5, 0.09375, (), jnp.float32)
    return dict(members=members, analysis=analysis, stencils=stencils, mixing=mixing)


smooth = 0.01
highest = lax.Precision.HIGHEST

def soft_abs(values):
    return jnp.sqrt(values * values + smooth)

def extend_field(field_block):
    margin = SPAN // 2
    wrapped = jnp.concatenate([field_block[:, -margin:], field_block, field_block[:, :margin]], axis=1)
    return jnp.pad(wrapped, ((margin, margin), (0, 0), (0, 0)))

def tap_sum(extended, weights):
    height = weights.shape[3]
    breadth = extended.shape[1] - SPAN + 1
    running = jnp.zeros((weights.shape[0], height, breadth, extended.shape[2]), jnp.float32)
    for row_tap in range(SPAN):
        for col_tap in range(SPAN):
            running = running + weights[:, row_tap, col_tap, :, None, None] * extended[None, row_tap:row_tap + height, col_tap:col_tap + breadth, :]
    return running

def reference(members, analysis, stencils, mixing):
    margin = SPAN // 2
    height = stencils.shape[3]
    padded = jnp.pad(stencils, ((0, 0), (0, 0), (0, 0), (margin, margin)))
    forward = padded[:, :, :, margin:margin + height]
    backward = jnp.stack([padded[:, SPAN - 1 - row_tap, ::-1, row_tap:row_tap + height] for row_tap in range(SPAN)], axis=1)

    def predict_single_member(member_index):
        mixed = jnp.einsum('bhwc,bco->hwo', tap_sum(extend_field(member_index), forward), mixing, precision=highest)
        bounded_activation = jnp.tanh(mixed)
        return (member_index + bounded_activation, bounded_activation)
    predicted_fields, bounded_activation = lax.map(predict_single_member, members)
    prediction_error = predicted_fields - analysis[None]

    def pair_step(other_member, totals):
        differ = prediction_error - lax.dynamic_index_in_dim(prediction_error, other_member, 0, keepdims=False)
        smooth_abs = soft_abs(differ)
        return (totals[0] + smooth_abs, totals[1] + differ / smooth_abs)
    zero_sums = jnp.zeros_like(prediction_error)
    sum_abs, sum_slope = lax.fori_loop(0, MEMBERS, pair_step, (zero_sums, zero_sums))
    own_abs = soft_abs(prediction_error)
    crps_field = lax.optimization_barrier(jnp.mean(own_abs, 0)) - lax.optimization_barrier(jnp.sum(sum_abs, 0)) / (2.0 * MEMBERS * (MEMBERS - 1))
    grad_out = prediction_error / own_abs - sum_slope / (MEMBERS - 1.0)
    inner_grad = grad_out * (1.0 - bounded_activation * bounded_activation)

    def adjoint_one(pair_args):
        outer_grad, inner_one = pair_args
        spread = tap_sum(extend_field(inner_one), backward)
        return outer_grad + jnp.einsum('bhwo,bco->hwc', spread, mixing, precision=highest)
    members_grad = lax.map(adjoint_one, (grad_out, inner_grad))
    return (members_grad, crps_field)
```

```python
import functools

import jax
import jax.numpy as jnp
from jax import lax
from jax.experimental import pallas as pl
from jax.experimental.pallas import tpu as pltpu
from jax.sharding import PartitionSpec as P

SMOOTH = 0.01
LANES = 16
TILE = 256


def split(value):
    high = value.astype(jnp.bfloat16)
    low = (value - high.astype(jnp.float32)).astype(jnp.bfloat16)
    return high, low


def product(left, right, axis):
    return lax.dot_general(
        left, right, (((1,), (axis,)), ((), ())), preferred_element_type=jnp.float32
    )


def product3(left_high, left_low, right_high, right_low, axis):
    rows = left_high.shape[0]
    both = product(jnp.concatenate([left_high, left_low], 0), right_high, axis)
    return both[:rows] + both[rows:] + product(left_high, right_low, axis)


def band_kernel(taps_ref, out_ref, *, margin, breadth):
    depth = taps_ref.shape[2]
    source = lax.broadcasted_iota(jnp.int32, (depth, TILE), 0)
    target = lax.broadcasted_iota(jnp.int32, (depth, TILE), 1)
    slot = target % LANES
    column = jnp.where(
        slot < breadth,
        slot,
        jnp.where(slot < breadth + margin, slot - breadth - margin, slot - margin),
    )
    column = jnp.where(slot < breadth + 2 * margin, column, 1000)
    same_row = (source // 8) == (target // LANES)
    for side in range(2):
        taps = taps_ref[side]
        for j in range(breadth):
            spread = (same_row & ((source % 8) == column - j + margin)).astype(jnp.float32)
            out_ref[side, :, j, :] = jnp.dot(
                taps, spread, precision=lax.Precision.HIGHEST, preferred_element_type=jnp.float32
            )


def mix_kernel(
    place_ref, core_ref, first_ref, second_ref, band_ref, mixing_ref, extra_ref,
    *rest, margin, blocks, axis, forward,
):
    outs, (high_ref, low_ref, shigh_ref, slow_ref, acc_ref) = rest[:-5], rest[-5:]
    step = pl.program_id(0)
    height = core_ref.shape[0]
    bases = band_ref.shape[0]
    channels = core_ref.shape[2]
    rows = height // blocks
    cells = rows * band_ref.shape[2]

    @pl.when(step == 0)
    def _():
        def fill(start, ref):
            count = ref.shape[0]
            value = ref[...].reshape(count * LANES, channels)
            high, low = split(value)
            at = pl.multiple_of(start * LANES, LANES)
            high_ref[pl.ds(at, count * LANES), :] = high
            low_ref[pl.ds(at, count * LANES), :] = low

        fill(margin, core_ref)
        fill(place_ref[0], first_ref)
        fill(place_ref[1], second_ref)
        for block in range(blocks):
            band = band_ref[:, block * rows : (block + 1) * rows].reshape(bases * cells, TILE)
            band_high, band_low = split(band)
            at = block * rows * LANES
            got = product3(
                band_high, band_low, high_ref[at : at + TILE, :], low_ref[at : at + TILE, :], 0
            )
            got_high, got_low = split(got)
            here = block * cells
            shigh_ref[:, here : here + cells, :] = got_high.reshape(bases, cells, channels)
            slow_ref[:, here : here + cells, :] = got_low.reshape(bases, cells, channels)
        acc_ref[...] = jnp.zeros_like(acc_ref)

    weight_high, weight_low = split(mixing_ref[0])
    acc_ref[...] += product3(shigh_ref[step], slow_ref[step], weight_high, weight_low, axis)

    @pl.when(step == pl.num_programs(0) - 1)
    def _():
        if forward:
            bounded = jnp.tanh(acc_ref[...])
            outs[0][...] = extra_ref[...] + bounded
            outs[1][...] = bounded
        else:
            outs[0][...] = extra_ref[...] + acc_ref[...]


def mix(place, core, first, second, band, mixing, extra, margin, blocks, forward):
    height, _, channels = core.shape
    bases = mixing.shape[0]
    total = extra.shape[0]
    whole = lambda a: pl.BlockSpec(a.shape, lambda b: (0,) * a.ndim)
    count = 2 if forward else 1
    out = jax.ShapeDtypeStruct((total, channels), jnp.float32)
    flops = 6 * total * channels * bases * (TILE + channels)
    return pl.pallas_call(
        functools.partial(
            mix_kernel, margin=margin, blocks=blocks, axis=0 if forward else 1, forward=forward
        ),
        grid=(bases,),
        out_shape=[out] * count,
        in_specs=[
            pl.BlockSpec(memory_space=pltpu.SMEM),
            whole(core), whole(first), whole(second), whole(band),
            pl.BlockSpec((1, channels, channels), lambda b: (b, 0, 0)),
            whole(extra),
        ],
        out_specs=[pl.BlockSpec((total, channels), lambda b: (0, 0))] * count,
        scratch_shapes=[
            pltpu.VMEM(((height + 2 * margin) * LANES, channels), jnp.bfloat16),
            pltpu.VMEM(((height + 2 * margin) * LANES, channels), jnp.bfloat16),
            pltpu.VMEM((bases, total, channels), jnp.bfloat16),
            pltpu.VMEM((bases, total, channels), jnp.bfloat16),
            pltpu.VMEM((total, channels), jnp.float32),
        ],
        cost_estimate=pl.CostEstimate(
            flops=flops, bytes_accessed=mixing.size * 4, transcendentals=0
        ),
        compiler_params=pltpu.CompilerParams(
            dimension_semantics=("arbitrary",), vmem_limit_bytes=40 << 20
        ),
        name="mix_forward" if forward else "mix_backward",
    )(place, core, first, second, band, mixing, extra)


def loss_kernel(half_ref, own_ref, other_ref, bounded_ref, mine_ref, theirs_ref, grad_ref, inner_ref, crps_ref):
    half = mine_ref.shape[1]
    me = half_ref[0]

    def slope(value):
        return value / jnp.sqrt(value * value + SMOOTH)

    def soft(value):
        return jnp.sqrt(value * value + SMOOTH)

    for part in range(2):
        at = slice(part * half, (part + 1) * half)
        analysis = jnp.where(me == part, mine_ref[...], theirs_ref[...])
        own = own_ref[:, at] - analysis
        differ = own - (other_ref[:, at] - analysis)
        grad = slope(own) - slope(differ)
        bounded = bounded_ref[:, at]
        grad_ref[:, at] = grad
        inner_ref[:, at] = grad * (1.0 - bounded * bounded)

        @pl.when(me == part)
        def _():
            other = other_ref[:, at] - mine_ref[...]
            first = own_ref[:, at] - mine_ref[...]
            gap = first - other
            pair = 2.0 * (soft(gap) + jnp.sqrt(jnp.full_like(gap, SMOOTH)))
            crps_ref[...] = 0.5 * (soft(first) + soft(other)) - pair / 4.0


def loss_pair(predicted, bounded, analysis, swapped_analysis):
    other = lax.ppermute(predicted, "ens", [(0, 1), (1, 0)])
    total, channels = predicted.shape
    full = jax.ShapeDtypeStruct((total, channels), jnp.float32)
    return pl.pallas_call(
        loss_kernel,
        out_shape=[full, full, jax.ShapeDtypeStruct(analysis.shape, jnp.float32)],
        in_specs=[pl.BlockSpec(memory_space=pltpu.SMEM)] + [pl.BlockSpec(memory_space=pltpu.VMEM)] * 5,
        out_specs=[pl.BlockSpec(memory_space=pltpu.VMEM)] * 3,
        compiler_params=pltpu.CompilerParams(vmem_limit_bytes=16 << 20),
        name="loss",
    )(lax.axis_index("ens").reshape(1), predicted, other, bounded, analysis, swapped_analysis)


def loss_many(predicted, bounded, analysis):
    grouped = lax.all_to_all(predicted[None], "ens", split_axis=2, concat_axis=0, tiled=True)
    misfit = grouped - analysis[None]
    count = misfit.shape[0]

    def step(other, totals):
        differ = misfit - lax.dynamic_index_in_dim(misfit, other, 0)
        smooth_abs = jnp.sqrt(differ * differ + SMOOTH)
        return totals[0] + smooth_abs.sum(0), totals[1] + differ / smooth_abs

    sums, slopes = lax.fori_loop(
        0, count, step, (jnp.zeros_like(misfit[0]), jnp.zeros_like(misfit))
    )
    own = jnp.sqrt(misfit * misfit + SMOOTH)
    crps = jnp.mean(own, 0) - sums / (2.0 * count * (count - 1))
    grad = misfit / own - slopes / (count - 1.0)
    grad = lax.all_to_all(grad, "ens", split_axis=0, concat_axis=2, tiled=True)[0]
    return grad, grad * (1.0 - bounded * bounded), crps


def ring_halo(field, margin):
    count = lax.axis_size("lon")
    up = [(i, (i + 1) % count) for i in range(count)]
    down = [(b, a) for a, b in up]
    breadth = field.shape[1]
    left = lax.ppermute(field[:, breadth - margin :], "lon", up)
    right = lax.ppermute(field[:, :margin], "lon", down)
    spare = jnp.zeros((field.shape[0], LANES - breadth - 2 * margin, field.shape[2]), field.dtype)
    return jnp.concatenate([field, left, right, spare], axis=1)


def swap_halo(core, margin):
    count = lax.axis_size("lat")
    odd = lax.axis_index("lat") % 2
    top = core.shape[0] - margin

    def swap(start, pairs):
        table = {i: i for i in range(count)}
        for low in pairs:
            if low + 1 < count:
                table[low], table[low + 1] = low + 1, low
        piece = lax.dynamic_slice_in_dim(core, start, margin, 0)
        return lax.ppermute(piece, "lat", sorted(table.items()))

    first = swap(jnp.where(odd == 0, top, 0), range(0, count, 2))
    second = swap(jnp.where(odd == 0, 0, top), range(1, count, 2))
    end = core.shape[0] + margin
    place = jnp.stack([jnp.where(odd == 0, end, 0), jnp.where(odd == 0, 0, end)]).astype(jnp.int32)
    return place, first, second


def tap_rows(taps, rows):
    bases, span, _, height = taps.shape
    window = TILE // LANES
    moved = jnp.transpose(taps, (0, 3, 1, 2))
    moved = jnp.pad(moved, ((0, 0), (0, 0), (0, 0), (0, 8 - span)))
    pieces = [
        jnp.pad(moved[:, i], ((0, 0), (i % rows, window - span - i % rows), (0, 0)))
        for i in range(height)
    ]
    return jnp.stack(pieces, 1).reshape(bases * height, window * 8)


def local(members, analysis, stencils, mixing):
    _, height, breadth, channels = members.shape
    bases, span = stencils.shape[:2]
    margin = span // 2
    blocks = next(
        n for n in range(1, height + 1)
        if height % n == 0 and height // n + 2 * margin <= TILE // LANES
    )
    rows = height // blocks
    members_total = lax.axis_size("ens")
    field = members[0]
    flat = analysis.reshape(height * breadth, analysis.shape[2])

    core = ring_halo(field, margin)
    if members_total == 2:
        swapped = lax.ppermute(flat, "ens", [(0, 1), (1, 0)])

    first_row = lax.axis_index("lat") * height
    padded = jnp.pad(stencils, ((0, 0), (0, 0), (0, 0), (margin, margin)))
    window = lax.dynamic_slice_in_dim(padded, first_row, height + 2 * margin, 3)
    reach = first_row + jnp.arange(height)[None] + jnp.arange(span)[:, None] - margin
    inside = (reach >= 0) & (reach < stencils.shape[3])
    forward = jnp.where(inside[None, :, None, :], window[:, :, :, margin : margin + height], 0.0)
    backward = jnp.stack(
        [window[:, span - 1 - tap, ::-1, tap : tap + height] for tap in range(span)], axis=1
    )
    taps = jnp.stack([tap_rows(forward, rows), tap_rows(backward, rows)])
    band = pl.pallas_call(
        functools.partial(band_kernel, margin=margin, breadth=breadth),
        out_shape=jax.ShapeDtypeStruct((2, bases * height, breadth, TILE), jnp.float32),
        in_specs=[pl.BlockSpec(memory_space=pltpu.VMEM)],
        out_specs=pl.BlockSpec(memory_space=pltpu.VMEM),
        name="band",
    )(taps).reshape(2, bases, height, breadth, TILE)

    place, first, second = swap_halo(core, margin)
    extra = field.reshape(height * breadth, channels)
    predicted, bounded = mix(
        place, core, first, second, band[0], mixing, extra, margin, blocks, True
    )
    if members_total == 2:
        grad, inner, crps = loss_pair(predicted, bounded, flat, swapped)
    else:
        grad, inner, crps = loss_many(predicted, bounded, flat)
    core = ring_halo(inner.reshape(height, breadth, channels), margin)
    place, first, second = swap_halo(core, margin)
    (result,) = mix(place, core, first, second, band[1], mixing, grad, margin, blocks, False)
    return (
        result.reshape(members.shape),
        crps.reshape(analysis.shape),
    )


def solution(mesh):
    in_specs = (P("ens", "lat", "lon", None), P("lat", "lon", "ens"), P(), P())
    out_specs = (P("ens", "lat", "lon", None), P("lat", "lon", "ens"))
    return jax.shard_map(local, mesh=mesh, in_specs=in_specs, out_specs=out_specs, check_vma=False)
```

```python
import functools

import jax
import jax.numpy as jnp
from jax import lax
from jax.experimental import pallas as pl
from jax.experimental.pallas import tpu as pltpu
from jax.sharding import PartitionSpec as P

SMOOTH = 0.01
SLOTS = 16
DEPTH = 256
EDGE = 256
VMEM = pl.BlockSpec(memory_space=pltpu.VMEM)
SMEM = pl.BlockSpec(memory_space=pltpu.SMEM)


def f32(*shape):
    return jax.ShapeDtypeStruct(shape, jnp.float32)


def b16(*shape):
    return jax.ShapeDtypeStruct(shape, jnp.bfloat16)


def split(value):
    high = value.astype(jnp.bfloat16)
    low = (value - high.astype(jnp.float32)).astype(jnp.bfloat16)
    return high, low


def product(left, right, axis):
    return lax.dot_general(
        left, right, (((1,), (axis,)), ((), ())), preferred_element_type=jnp.float32
    )


def product3(left_high, left_low, right_high, right_low, axis):
    rows = left_high.shape[0]
    both = product(jnp.concatenate([left_high, left_low], 0), right_high, axis)
    return both[:rows] + both[rows:] + product(left_high, right_low, axis)


def call(body, name, out_shape, operands, specs=None, scratch=(), flops=0, size=0, limit=24):
    return pl.pallas_call(
        body,
        out_shape=out_shape,
        in_specs=specs or [VMEM] * len(operands),
        out_specs=[VMEM] * len(out_shape),
        scratch_shapes=scratch,
        cost_estimate=pl.CostEstimate(flops=flops, bytes_accessed=size, transcendentals=0),
        compiler_params=pltpu.CompilerParams(vmem_limit_bytes=limit << 20),
        name=name,
    )(*operands)


def band_kernel(place_ref, stencils_ref, high_ref, low_ref, table_ref, band_ref, *, rows, forward):
    bases, span, _, total = stencils_ref.shape
    blocks = high_ref.shape[0]
    margin = span // 2
    breadth = high_ref.shape[1] // (bases * rows)
    first_row = place_ref[0]
    iota = lambda shape, axis: lax.broadcasted_iota(jnp.int32, shape, axis)

    table_ref[...] = jnp.zeros_like(table_ref)
    for base in range(bases):
        for tap in range(span):
            at = (base * 8 + tap) * 8
            table_ref[at : at + span, :total] = stencils_ref[base, tap]
    table = split(table_ref[...])

    group = blocks * SLOTS
    shifts = [margin] if forward else list(range(span))
    count = group * len(shifts)
    line, latitude = iota((count, table_ref.shape[1]), 0), iota((count, table_ref.shape[1]), 1)
    local_row = line % SLOTS
    shift = shifts[0] if forward else line // group
    wanted = first_row + (line % group) // SLOTS * rows + local_row + shift - margin
    picks = ((latitude == wanted) & (local_row < rows)).astype(jnp.float32).astype(jnp.bfloat16)

    width = table_ref.shape[0]
    tap_of = iota((group, width), 1) // 8 % 8
    stacked = []
    for part in table:
        picked = product(picks, part, 1)
        if forward:
            line = iota((group, width), 0)
            reach = first_row + line // SLOTS * rows + line % SLOTS + tap_of - margin
            taps = jnp.where((reach >= 0) & (reach < total), picked, 0.0)
        else:
            taps = jnp.zeros((group, width), jnp.float32)
            for tap in range(span):
                here = picked[tap * group : (tap + 1) * group]
                taps = jnp.where(tap_of == span - 1 - tap, here, taps)
        stacked += [taps[:, at : at + 128] for at in range(0, width, 128)]
    left = jnp.concatenate(stacked, 0).astype(jnp.bfloat16)
    pairs = width // 128

    source, target = iota((128, 256), 0), iota((128, 256), 1)
    slot = target % SLOTS
    column = jnp.where(
        slot < breadth,
        slot,
        jnp.where(slot < breadth + margin, slot - breadth - margin, slot - margin),
    )
    row_tap, column_tap = source // 8 % 8, source % 8
    to_row = target % 128 // SLOTS
    if not forward:
        row_tap, column_tap = span - 1 - row_tap, span - 1 - column_tap
    same = (row_tap == to_row) & (source // 64 == target // 128) & (slot < breadth + 2 * margin)
    same = same & (source % 8 < span) & (source // 8 % 8 < span)
    offset = jnp.where(same, column_tap - column, 1000)
    zeros = jnp.zeros((left.shape[0], 128), jnp.float32)
    for j in range(breadth):
        spread = (offset == margin - j).astype(jnp.float32).astype(jnp.bfloat16)
        both = product(left, spread, 0)
        for odd in range(2):
            wide = jnp.concatenate([both[:, odd * 128 : odd * 128 + 128], zeros], 1)
            wide = pltpu.roll(wide, 0, 1, stride=SLOTS, stride_axis=0)
            for part in range(2):
                for pair in range(pairs):
                    base = 2 * pair + odd
                    if base >= bases:
                        continue
                    for block in range(blocks):
                        at = ((part * pairs + pair) * blocks + block) * SLOTS
                        lines = pl.ds(base * rows * breadth + j, rows, stride=breadth)
                        for half in range(2):
                            band_ref[part, half, block, lines, :] = wide[
                                at : at + rows, half * 128 : half * 128 + 128
                            ]
    for half in range(2):
        lanes = slice(half * 128, half * 128 + 128)
        high_ref[:, :, lanes] = band_ref[0, half].astype(jnp.bfloat16)
        low_ref[:, :, lanes] = band_ref[1, half].astype(jnp.bfloat16)


def bands(place, stencils, rows, blocks, breadth, forward):
    bases, span, _, total = stencils.shape
    lines = bases * rows * breadth
    return call(
        functools.partial(band_kernel, rows=rows, forward=forward),
        "band_forward" if forward else "band_backward",
        [b16(blocks, lines, DEPTH)] * 2,
        [place, stencils],
        [SMEM, VMEM],
        [
            pltpu.VMEM(((bases + 1) // 2 * 128, -(-total // 128) * 128), jnp.float32),
            pltpu.VMEM((2, DEPTH // 128, blocks, lines, 128), jnp.float32),
        ],
        flops=10**9, size=4 << 20,
    )


def pack_sides(field_ref, up_ref, down_ref, breadth):
    height = field_ref.shape[0] // breadth
    margin = up_ref.shape[0] // height
    for row in range(height):
        at = slice(row * margin, (row + 1) * margin)
        up_ref[at, :] = field_ref[(row + 1) * breadth - margin : (row + 1) * breadth, :]
        down_ref[at, :] = field_ref[row * breadth : row * breadth + margin, :]


def sides(flat, breadth, margin):
    shape = f32(flat.shape[0] // breadth * margin, flat.shape[1])
    return call(
        functools.partial(pack_sides, breadth=breadth), "sides", [shape] * 2, [flat],
        size=1 << 20, limit=8,
    )


def assemble_kernel(place_ref, field_ref, left_ref, right_ref, wide_ref, first_ref, second_ref, *, breadth):
    height = field_ref.shape[0] // breadth
    margin = left_ref.shape[0] // height
    spare = jnp.zeros((SLOTS - breadth - 2 * margin, field_ref.shape[1]), jnp.float32)
    for row in range(height):
        at = row * SLOTS
        here = slice(row * margin, (row + 1) * margin)
        wide_ref[at : at + breadth, :] = field_ref[row * breadth : (row + 1) * breadth, :]
        wide_ref[at + breadth : at + SLOTS, :] = jnp.concatenate(
            [left_ref[here, :], right_ref[here, :], spare], 0
        )
    low = wide_ref[: margin * SLOTS, :]
    high = wide_ref[(height - margin) * SLOTS :, :]
    odd = place_ref[1] == 1
    first_ref[...] = jnp.where(odd, low, high)
    second_ref[...] = jnp.where(odd, high, low)


def assemble(place, flat, left, right, breadth):
    cells, channels = flat.shape
    height = cells // breadth
    edge = f32(left.shape[0] // height * SLOTS, channels)
    return call(
        functools.partial(assemble_kernel, breadth=breadth), "assemble",
        [f32(height * SLOTS, channels), edge, edge],
        [place, flat, left, right], [SMEM, VMEM, VMEM, VMEM], size=2 << 20, limit=8,
    )


def ring(up, down):
    count = lax.axis_size("lon")
    there = [(i, (i + 1) % count) for i in range(count)]
    back = [(b, a) for a, b in there]
    return lax.ppermute(up, "lon", there), lax.ppermute(down, "lon", back)


def swap(first, second):
    count = lax.axis_size("lat")

    def one(piece, lows):
        table = {i: i for i in range(count)}
        for low in lows:
            if low + 1 < count:
                table[low], table[low + 1] = low + 1, low
        return lax.ppermute(piece, "lat", sorted(table.items()))

    return one(first, range(0, count, 2)), one(second, range(1, count, 2))


def stencil(place_ref, wide_ref, first_ref, second_ref, bhigh_ref, blow_ref, shigh_ref, slow_ref, xhigh_ref, xlow_ref):
    bases, total, channels = shigh_ref.shape
    blocks = bhigh_ref.shape[0]
    cells = total // blocks

    def fill(at, ref):
        high, low = split(ref[...])
        xhigh_ref[pl.ds(at, ref.shape[0]), :] = high
        xlow_ref[pl.ds(at, ref.shape[0]), :] = low

    edge = first_ref.shape[0]
    fill(edge, wide_ref)
    fill(pl.multiple_of(place_ref[2], SLOTS), first_ref)
    fill(pl.multiple_of(place_ref[3], SLOTS), second_ref)
    stride = (wide_ref.shape[0]) // blocks
    for block in range(blocks):
        window = slice(block * stride, block * stride + DEPTH)
        got = product3(bhigh_ref[block], blow_ref[block], xhigh_ref[window], xlow_ref[window], 0)
        high, low = split(got)
        here = slice(block * cells, (block + 1) * cells)
        shigh_ref[:, here, :] = high.reshape(bases, cells, channels)
        slow_ref[:, here, :] = low.reshape(bases, cells, channels)


def contract(shigh_ref, slow_ref, mixing_ref, acc_ref, lanes, axis):
    acc_ref[...] = jnp.zeros_like(acc_ref)

    def step(base, _):
        weight_high, weight_low = split(mixing_ref[base, :, lanes])
        acc_ref[...] += product3(shigh_ref[base], slow_ref[base], weight_high, weight_low, axis)

    lax.fori_loop(0, mixing_ref.shape[0], step, None)


def forward_first(place_ref, wide_ref, first_ref, second_ref, bhigh_ref, blow_ref, mixing_ref, field_ref,
                  predicted_ref, bounded_ref, shigh_ref, slow_ref, xhigh_ref, xlow_ref, acc_ref):
    stencil(place_ref, wide_ref, first_ref, second_ref, bhigh_ref, blow_ref, shigh_ref, slow_ref, xhigh_ref, xlow_ref)
    lanes = slice(0, acc_ref.shape[1])
    contract(shigh_ref, slow_ref, mixing_ref, acc_ref, lanes, 0)
    bounded = jnp.tanh(acc_ref[...])
    bounded_ref[...] = bounded
    predicted_ref[...] = field_ref[:, lanes] + bounded


def forward_rest(shigh_ref, slow_ref, mixing_ref, field_ref, predicted_ref, bounded_ref, acc_ref):
    lanes = slice(field_ref.shape[1] - acc_ref.shape[1], field_ref.shape[1])
    contract(shigh_ref, slow_ref, mixing_ref, acc_ref, lanes, 0)
    bounded = jnp.tanh(acc_ref[...])
    bounded_ref[...] = bounded
    predicted_ref[...] = field_ref[:, lanes] + bounded


def backward_all(place_ref, wide_ref, first_ref, second_ref, bhigh_ref, blow_ref, mixing_ref, grad_ref, tail_ref,
                 out_ref, shigh_ref, slow_ref, xhigh_ref, xlow_ref, acc_ref):
    stencil(place_ref, wide_ref, first_ref, second_ref, bhigh_ref, blow_ref, shigh_ref, slow_ref, xhigh_ref, xlow_ref)
    contract(shigh_ref, slow_ref, mixing_ref, acc_ref, slice(None), 1)
    edge = grad_ref.shape[1]
    out_ref[:, :edge] = acc_ref[:, :edge] + grad_ref[...]
    out_ref[:, edge:] = acc_ref[:, edge:] + tail_ref[...]


def slope(value):
    return value * lax.rsqrt(value * value + SMOOTH)


def soft(value):
    return jnp.sqrt(value * value + SMOOTH)


def loss_first(own_ref, other_ref, bounded_ref, analysis_ref, grad_ref, inner_ref):
    analysis = analysis_ref[:, : own_ref.shape[1]]
    own = own_ref[...] - analysis
    grad = slope(own) - slope(own - (other_ref[...] - analysis))
    grad_ref[...] = grad
    inner_ref[...] = grad * (1.0 - bounded_ref[...] * bounded_ref[...])


def loss_rest(own_ref, other_ref, bounded_ref, analysis_ref, before_ref, grad_ref, inner_ref, up_ref, down_ref, *, breadth):
    edge = before_ref.shape[1]
    analysis = analysis_ref[:, edge:]
    own = own_ref[...] - analysis
    grad = slope(own) - slope(own - (other_ref[...] - analysis))
    grad_ref[...] = grad
    inner_ref[:, :edge] = before_ref[...]
    inner_ref[:, edge:] = grad * (1.0 - bounded_ref[...] * bounded_ref[...])
    pack_sides(inner_ref, up_ref, down_ref, breadth)


def whole_analysis(place_ref, mine_ref, theirs_ref, out_ref):
    half = mine_ref.shape[1]
    first = place_ref[4] == 0
    mine, theirs = mine_ref[...], theirs_ref[...]
    out_ref[:, :half] = jnp.where(first, mine, theirs)
    out_ref[:, half:] = jnp.where(first, theirs, mine)


def crps_kernel(place_ref, own1_ref, own2_ref, other1_ref, other2_ref, mine_ref, out_ref):
    half = mine_ref.shape[1]
    edge = own1_ref.shape[1]
    for part in range(2):
        @pl.when(place_ref[4] == part)
        def _():
            low, high = part * half, (part + 1) * half
            pieces = []
            if low < edge:
                pieces.append((own1_ref, other1_ref, slice(low, min(high, edge)), 0))
            if high > edge:
                start = max(low, edge)
                pieces.append((own2_ref, other2_ref, slice(start - edge, high - edge), start - low))
            for own_ref, other_ref, lanes, at in pieces:
                here = slice(at, at + lanes.stop - lanes.start)
                mine = mine_ref[:, here]
                own = own_ref[:, lanes] - mine
                other = other_ref[:, lanes] - mine
                gap = own - other
                pair = 2.0 * (soft(gap) + jnp.sqrt(jnp.full_like(gap, SMOOTH)))
                out_ref[:, here] = 0.5 * (soft(own) + soft(other)) - pair / 4.0


def loss_many(predicted, bounded, analysis):
    grouped = lax.all_to_all(predicted[None], "ens", split_axis=2, concat_axis=0, tiled=True)
    misfit = grouped - analysis[None]
    count = misfit.shape[0]

    def step(other, totals):
        differ = misfit - lax.dynamic_index_in_dim(misfit, other, 0)
        smooth_abs = jnp.sqrt(differ * differ + SMOOTH)
        return totals[0] + smooth_abs.sum(0), totals[1] + differ / smooth_abs

    sums, slopes = lax.fori_loop(
        0, count, step, (jnp.zeros_like(misfit[0]), jnp.zeros_like(misfit))
    )
    own = jnp.sqrt(misfit * misfit + SMOOTH)
    crps = jnp.mean(own, 0) - sums / (2.0 * count * (count - 1))
    grad = misfit / own - slopes / (count - 1.0)
    grad = lax.all_to_all(grad, "ens", split_axis=0, concat_axis=2, tiled=True)[0]
    return grad, grad * (1.0 - bounded * bounded), crps


def local(members, analysis, stencils, mixing):
    _, height, breadth, channels = members.shape
    bases, span = stencils.shape[:2]
    margin = span // 2
    blocks = next(
        n for n in range(1, height + 1)
        if height % n == 0 and height // n + 2 * margin <= DEPTH // SLOTS
    )
    rows = height // blocks
    cells = height * breadth
    pair = lax.axis_size("ens") == 2
    flat = members.reshape(cells, channels)
    mine = analysis.reshape(cells, analysis.shape[2])

    odd = lax.axis_index("lat") % 2
    end = (height + margin) * SLOTS
    place = jnp.stack([
        lax.axis_index("lat") * height, odd, (1 - odd) * end, odd * end, lax.axis_index("ens")
    ]).astype(jnp.int32)

    left, right = ring(*sides(flat, breadth, margin))
    if pair:
        theirs = lax.ppermute(mine, "ens", [(0, 1), (1, 0)])
    band = bands(place, stencils, rows, blocks, breadth, True)
    wide, first, second = assemble(place, flat, left, right, breadth)
    first, second = swap(first, second)

    window = pltpu.VMEM(((height + 2 * margin) * SLOTS, channels), jnp.bfloat16)
    taps = [b16(bases, cells, channels)] * 2
    stencil_flops = 6 * blocks * bases * rows * breadth * DEPTH * channels
    mix_flops = 6 * cells * bases * channels * channels
    rest = channels - EDGE
    predicted1, bounded1, shigh, slow = call(
        forward_first, "forward_first", [f32(cells, EDGE)] * 2 + taps,
        [place, wide, first, second, *band, mixing, flat], [SMEM] + [VMEM] * 7,
        [window, window, pltpu.VMEM((cells, EDGE), jnp.float32)],
        flops=stencil_flops + mix_flops * EDGE // channels,
    )
    if pair:
        other1 = lax.ppermute(predicted1, "ens", [(0, 1), (1, 0)])
    predicted2, bounded2 = call(
        forward_rest, "forward_rest", [f32(cells, rest)] * 2, [shigh, slow, mixing, flat],
        scratch=[pltpu.VMEM((cells, rest), jnp.float32)], flops=mix_flops * rest // channels,
    )
    back = bands(place, stencils, rows, blocks, breadth, False)
    if pair:
        other2 = lax.ppermute(predicted2, "ens", [(0, 1), (1, 0)])
        (known,) = call(
            whole_analysis, "whole_analysis", [f32(cells, channels)], [place, mine, theirs],
            [SMEM, VMEM, VMEM], size=1 << 20, limit=8,
        )
        grad1, inner1 = call(
            loss_first, "loss_first", [f32(cells, EDGE)] * 2,
            [predicted1, other1, bounded1, known], size=1 << 20, limit=8,
        )
        side = f32(height * margin, channels)
        grad2, inner, up, down = call(
            functools.partial(loss_rest, breadth=breadth), "loss_rest",
            [f32(cells, rest), f32(cells, channels), side, side],
            [predicted2, other2, bounded2, known, inner1], size=2 << 20, limit=8,
        )
        (crps,) = call(
            crps_kernel, "crps", [f32(*mine.shape)],
            [place, predicted1, predicted2, other1, other2, mine], [SMEM] + [VMEM] * 5,
            size=1 << 20, limit=8,
        )
    else:
        predicted = jnp.concatenate([predicted1, predicted2], 1)
        bounded = jnp.concatenate([bounded1, bounded2], 1)
        grad, inner, crps = loss_many(predicted, bounded, mine)
        grad1, grad2 = grad[:, :EDGE], grad[:, EDGE:]
        up, down = sides(inner, breadth, margin)

    left, right = ring(up, down)
    wide, first, second = assemble(place, inner, left, right, breadth)
    first, second = swap(first, second)
    (result,) = call(
        backward_all, "backward_all", [f32(cells, channels)],
        [place, wide, first, second, *back, mixing, grad1, grad2], [SMEM] + [VMEM] * 8,
        [pltpu.VMEM(s.shape, s.dtype) for s in taps]
        + [window, window, pltpu.VMEM((cells, channels), jnp.float32)],
        flops=stencil_flops + mix_flops,
    )
    return result.reshape(members.shape), crps.reshape(analysis.shape)


def solution(mesh):
    in_specs = (P("ens", "lat", "lon", None), P("lat", "lon", "ens"), P(), P())
    out_specs = (P("ens", "lat", "lon", None), P("lat", "lon", "ens"))
    return jax.shard_map(local, mesh=mesh, in_specs=in_specs, out_specs=out_specs, check_vma=False)
```

```python
import functools

import jax
import jax.numpy as jnp
from jax import lax
from jax.experimental import pallas as pl
from jax.experimental.pallas import tpu as pltpu
from jax.sharding import PartitionSpec as P


SMOOTH = 0.01
SLOTS = 16
DEPTH = 256
EDGE = 256
SWAP = [(0, 1), (1, 0)]
VMEM = pl.BlockSpec(memory_space=pltpu.VMEM)
SMEM = pl.BlockSpec(memory_space=pltpu.SMEM)


def f32(*shape):
    return jax.ShapeDtypeStruct(shape, jnp.float32)


def b16(*shape):
    return jax.ShapeDtypeStruct(shape, jnp.bfloat16)


def split(value):
    high = value.astype(jnp.bfloat16)
    low = (value - high.astype(jnp.float32)).astype(jnp.bfloat16)
    return high, low


def product(left, right, axis):
    return lax.dot_general(
        left, right, (((1,), (axis,)), ((), ())), preferred_element_type=jnp.float32
    )


def product3(left_high, left_low, right_high, right_low, axis):
    rows = left_high.shape[0]
    both = product(jnp.concatenate([left_high, left_low], 0), right_high, axis)
    return both[:rows] + both[rows:] + product(left_high, right_low, axis)


def call(body, out_shape, operands, specs=None, scratch=(), flops=0, size=0, limit=12):
    return pl.pallas_call(
        body,
        out_shape=out_shape,
        in_specs=specs or [VMEM] * len(operands),
        out_specs=[VMEM] * len(out_shape),
        scratch_shapes=scratch,
        cost_estimate=pl.CostEstimate(flops=flops, bytes_accessed=size, transcendentals=0),
        compiler_params=pltpu.CompilerParams(vmem_limit_bytes=limit << 20),
    )(*operands)


def band_kernel(place_ref, stencils_ref, high_ref, low_ref, table_ref, band_ref, *, rows, forward):
    bases, span, _, total = stencils_ref.shape
    blocks = high_ref.shape[0]
    margin = span // 2
    breadth = high_ref.shape[1] // (bases * rows)
    first_row = place_ref[0]
    iota = lambda shape, axis: lax.broadcasted_iota(jnp.int32, shape, axis)

    table_ref[...] = jnp.zeros_like(table_ref)
    for base in range(bases):
        for tap in range(span):
            at = (base * 8 + tap) * 8
            table_ref[at : at + span, :total] = stencils_ref[base, tap]
    table = split(table_ref[...])

    group = blocks * SLOTS
    shifts = [margin] if forward else list(range(span))
    count = group * len(shifts)
    line, latitude = iota((count, table_ref.shape[1]), 0), iota((count, table_ref.shape[1]), 1)
    local_row = line % SLOTS
    shift = shifts[0] if forward else line // group
    wanted = first_row + (line % group) // SLOTS * rows + local_row + shift - margin
    picks = ((latitude == wanted) & (local_row < rows)).astype(jnp.float32).astype(jnp.bfloat16)

    width = table_ref.shape[0]
    tap_of = iota((group, width), 1) // 8 % 8
    stacked = []
    for part in table:
        picked = product(picks, part, 1)
        if forward:
            line = iota((group, width), 0)
            reach = first_row + line // SLOTS * rows + line % SLOTS + tap_of - margin
            taps = jnp.where((reach >= 0) & (reach < total), picked, 0.0)
        else:
            taps = jnp.zeros((group, width), jnp.float32)
            for tap in range(span):
                here = picked[tap * group : (tap + 1) * group]
                taps = jnp.where(tap_of == span - 1 - tap, here, taps)
        stacked += [taps[:, at : at + 128] for at in range(0, width, 128)]
    left = jnp.concatenate(stacked, 0).astype(jnp.bfloat16)
    pairs = width // 128

    source, target = iota((128, 256), 0), iota((128, 256), 1)
    slot = target % SLOTS
    column = jnp.where(
        slot < breadth,
        slot,
        jnp.where(slot < breadth + margin, slot - breadth - margin, slot - margin),
    )
    row_tap, column_tap = source // 8 % 8, source % 8
    to_row = target % 128 // SLOTS
    if not forward:
        row_tap, column_tap = span - 1 - row_tap, span - 1 - column_tap
    same = (row_tap == to_row) & (source // 64 == target // 128) & (slot < breadth + 2 * margin)
    same = same & (source % 8 < span) & (source // 8 % 8 < span)
    offset = jnp.where(same, column_tap - column, 1000)
    zeros = jnp.zeros((left.shape[0], 128), jnp.float32)
    for j in range(breadth):
        spread = (offset == margin - j).astype(jnp.float32).astype(jnp.bfloat16)
        both = product(left, spread, 0)
        for odd in range(2):
            wide = jnp.concatenate([both[:, odd * 128 : odd * 128 + 128], zeros], 1)
            wide = pltpu.roll(wide, 0, 1, stride=SLOTS, stride_axis=0)
            for part in range(2):
                for pair in range(pairs):
                    base = 2 * pair + odd
                    if base >= bases:
                        continue
                    for block in range(blocks):
                        at = ((part * pairs + pair) * blocks + block) * SLOTS
                        lines = pl.ds(base * rows * breadth + j, rows, stride=breadth)
                        for half in range(2):
                            band_ref[part, half, block, lines, :] = wide[
                                at : at + rows, half * 128 : half * 128 + 128
                            ]
    for half in range(2):
        lanes = slice(half * 128, half * 128 + 128)
        high_ref[:, :, lanes] = band_ref[0, half].astype(jnp.bfloat16)
        low_ref[:, :, lanes] = band_ref[1, half].astype(jnp.bfloat16)


def bands(place, stencils, rows, blocks, breadth, forward):
    bases, _, _, total = stencils.shape
    lines = bases * rows * breadth
    return call(
        functools.partial(band_kernel, rows=rows, forward=forward),
        [b16(blocks, lines, DEPTH)] * 2,
        [place, stencils],
        [SMEM, VMEM],
        [
            pltpu.VMEM(((bases + 1) // 2 * 128, -(-total // 128) * 128), jnp.float32),
            pltpu.VMEM((2, DEPTH // 128, blocks, lines, 128), jnp.float32),
        ],
        flops=10**9, size=4 << 20,
    )


def pack_sides(field_ref, up_ref, down_ref, breadth):
    height = field_ref.shape[0] // breadth
    margin = up_ref.shape[0] // height
    for row in range(height):
        at = slice(row * margin, (row + 1) * margin)
        up_ref[at, :] = field_ref[(row + 1) * breadth - margin : (row + 1) * breadth, :]
        down_ref[at, :] = field_ref[row * breadth : row * breadth + margin, :]


def keep_sides(field_ref, up_ref, down_ref, kept_ref, *, breadth):
    pack_sides(field_ref, up_ref, down_ref, breadth)
    kept_ref[...] = field_ref[...]


def sides(flat, breadth, margin):
    shape = f32(flat.shape[0] // breadth * margin, flat.shape[1])
    return call(
        functools.partial(keep_sides, breadth=breadth), [shape, shape, f32(*flat.shape)],
        [flat], size=1 << 20, limit=8,
    )


def assemble_kernel(place_ref, field_ref, left_ref, right_ref, wide_ref, first_ref, second_ref, *, breadth):
    height = field_ref.shape[0] // breadth
    margin = left_ref.shape[0] // height
    spare = jnp.zeros((SLOTS - breadth - 2 * margin, field_ref.shape[1]), jnp.float32)
    for row in range(height):
        at = row * SLOTS
        here = slice(row * margin, (row + 1) * margin)
        wide_ref[at : at + breadth, :] = field_ref[row * breadth : (row + 1) * breadth, :]
        wide_ref[at + breadth : at + SLOTS, :] = jnp.concatenate(
            [left_ref[here, :], right_ref[here, :], spare], 0
        )
    low = wide_ref[: margin * SLOTS, :]
    high = wide_ref[(height - margin) * SLOTS :, :]
    odd = place_ref[1] == 1
    first_ref[...] = jnp.where(odd, low, high)
    second_ref[...] = jnp.where(odd, high, low)


def assemble(place, flat, left, right, breadth):
    cells, channels = flat.shape
    height = cells // breadth
    edge = f32(left.shape[0] // height * SLOTS, channels)
    return call(
        functools.partial(assemble_kernel, breadth=breadth),
        [f32(height * SLOTS, channels), edge, edge],
        [place, flat, left, right], [SMEM, VMEM, VMEM, VMEM], size=2 << 20, limit=8,
    )


def ring(up, down):
    count = lax.axis_size("lon")
    there = [(i, (i + 1) % count) for i in range(count)]
    back = [(b, a) for a, b in there]
    return lax.ppermute(up, "lon", there), lax.ppermute(down, "lon", back)


def swap(first, second):
    count = lax.axis_size("lat")

    def one(piece, lows):
        table = {i: i for i in range(count)}
        for low in lows:
            if low + 1 < count:
                table[low], table[low + 1] = low + 1, low
        return lax.ppermute(piece, "lat", sorted(table.items()))

    return (one(first, range(0, count, 2)), one(second, range(1, count, 2)))


def stencil(place_ref, wide_ref, first_ref, second_ref, bhigh_ref, blow_ref, shigh_ref, slow_ref, xhigh_ref, xlow_ref):
    bases, total, channels = shigh_ref.shape
    blocks = bhigh_ref.shape[0]
    cells = total // blocks

    def fill(at, ref):
        high, low = split(ref[...])
        xhigh_ref[pl.ds(at, ref.shape[0]), :] = high
        xlow_ref[pl.ds(at, ref.shape[0]), :] = low

    edge = first_ref.shape[0]
    fill(edge, wide_ref)
    fill(pl.multiple_of(place_ref[2], SLOTS), first_ref)
    fill(pl.multiple_of(place_ref[3], SLOTS), second_ref)
    stride = (wide_ref.shape[0]) // blocks
    for block in range(blocks):
        window = slice(block * stride, block * stride + DEPTH)
        got = product3(bhigh_ref[block], blow_ref[block], xhigh_ref[window], xlow_ref[window], 0)
        high, low = split(got)
        here = slice(block * cells, (block + 1) * cells)
        shigh_ref[:, here, :] = high.reshape(bases, cells, channels)
        slow_ref[:, here, :] = low.reshape(bases, cells, channels)


def load_mixing(place_ref, mixing_ref, high_ref, low_ref, wide_ref, sem_ref):
    bases, slots = mixing_ref.shape[0], wide_ref.shape[0]

    def copy(base):
        slot = base % slots
        return pltpu.make_async_copy(mixing_ref.at[base], wide_ref.at[slot], sem_ref.at[slot])

    for base in range(min(slots, bases)):
        copy(base).start()
    for base in range(bases):
        copy(base).wait()
        high_ref[base], low_ref[base] = split(wide_ref[base % slots])
        if base + slots < bases:
            copy(base + slots).start()


def contract(shigh_ref, slow_ref, mhigh_ref, mlow_ref, lanes, axis):
    total = None
    for base in range(mhigh_ref.shape[0]):
        part = product3(
            shigh_ref[base], slow_ref[base], mhigh_ref[base, :, lanes], mlow_ref[base, :, lanes], axis
        )
        total = part if total is None else total + part
    return total


def finish(total, field_ref, lanes, predicted_ref, bounded_ref):
    bounded = jnp.tanh(total)
    bounded_ref[...] = bounded
    predicted_ref[...] = field_ref[:, lanes] + bounded


def forward_first(place_ref, wide_ref, first_ref, second_ref, bhigh_ref, blow_ref, mhigh_ref, mlow_ref, field_ref,
                  predicted_ref, bounded_ref, shigh_ref, slow_ref, xhigh_ref, xlow_ref):
    stencil(place_ref, wide_ref, first_ref, second_ref, bhigh_ref, blow_ref, shigh_ref, slow_ref, xhigh_ref, xlow_ref)
    lanes = slice(0, predicted_ref.shape[1])
    total = contract(shigh_ref, slow_ref, mhigh_ref, mlow_ref, lanes, 0)
    finish(total, field_ref, lanes, predicted_ref, bounded_ref)


def forward_rest(shigh_ref, slow_ref, mhigh_ref, mlow_ref, field_ref, predicted_ref, bounded_ref):
    lanes = slice(field_ref.shape[1] - predicted_ref.shape[1], field_ref.shape[1])
    total = contract(shigh_ref, slow_ref, mhigh_ref, mlow_ref, lanes, 0)
    finish(total, field_ref, lanes, predicted_ref, bounded_ref)


def backward_all(place_ref, wide_ref, first_ref, second_ref, bhigh_ref, blow_ref, mhigh_ref, mlow_ref, grad_ref, tail_ref,
                 out_ref, shigh_ref, slow_ref, xhigh_ref, xlow_ref):
    stencil(place_ref, wide_ref, first_ref, second_ref, bhigh_ref, blow_ref, shigh_ref, slow_ref, xhigh_ref, xlow_ref)
    total = contract(shigh_ref, slow_ref, mhigh_ref, mlow_ref, slice(None), 1)
    edge = grad_ref.shape[1]
    out_ref[:, :edge] = total[:, :edge] + grad_ref[...]
    out_ref[:, edge:] = total[:, edge:] + tail_ref[...]


def slope(value):
    return value * lax.rsqrt(value * value + SMOOTH)


def soft(value):
    return jnp.sqrt(value * value + SMOOTH)


def loss_first(own_ref, other_ref, bounded_ref, analysis_ref, grad_ref, inner_ref):
    analysis = analysis_ref[:, : own_ref.shape[1]]
    own = own_ref[...] - analysis
    grad = slope(own) - slope(own - (other_ref[...] - analysis))
    grad_ref[...] = grad
    inner_ref[...] = grad * (1.0 - bounded_ref[...] * bounded_ref[...])


def loss_rest(own_ref, other_ref, bounded_ref, analysis_ref, before_ref, grad_ref, inner_ref, up_ref, down_ref, *, breadth):
    edge = before_ref.shape[1]
    analysis = analysis_ref[:, edge:]
    own = own_ref[...] - analysis
    grad = slope(own) - slope(own - (other_ref[...] - analysis))
    grad_ref[...] = grad
    inner_ref[:, :edge] = before_ref[...]
    inner_ref[:, edge:] = grad * (1.0 - bounded_ref[...] * bounded_ref[...])
    pack_sides(inner_ref, up_ref, down_ref, breadth)


def whole_analysis(place_ref, mine_ref, theirs_ref, out_ref):
    half = mine_ref.shape[1]
    first = place_ref[4] == 0
    mine, theirs = mine_ref[...], theirs_ref[...]
    out_ref[:, :half] = jnp.where(first, mine, theirs)
    out_ref[:, half:] = jnp.where(first, theirs, mine)


def crps_kernel(place_ref, own1_ref, own2_ref, other1_ref, other2_ref, mine_ref, out_ref):
    half = mine_ref.shape[1]
    edge = own1_ref.shape[1]
    for part in range(2):
        @pl.when(place_ref[4] == part)
        def _():
            low, high = part * half, (part + 1) * half
            pieces = []
            if low < edge:
                pieces.append((own1_ref, other1_ref, slice(low, min(high, edge)), 0))
            if high > edge:
                start = max(low, edge)
                pieces.append((own2_ref, other2_ref, slice(start - edge, high - edge), start - low))
            for own_ref, other_ref, lanes, at in pieces:
                here = slice(at, at + lanes.stop - lanes.start)
                mine = mine_ref[:, here]
                own = own_ref[:, lanes] - mine
                other = other_ref[:, lanes] - mine
                gap = own - other
                pair = 2.0 * (soft(gap) + jnp.sqrt(jnp.full_like(gap, SMOOTH)))
                out_ref[:, here] = 0.5 * (soft(own) + soft(other)) - pair / 4.0


def loss_many(predicted, bounded, analysis):
    grouped = lax.all_to_all(predicted[None], "ens", split_axis=2, concat_axis=0, tiled=True)
    misfit = grouped - analysis[None]
    count = misfit.shape[0]

    def step(other, totals):
        differ = misfit - lax.dynamic_index_in_dim(misfit, other, 0)
        smooth_abs = jnp.sqrt(differ * differ + SMOOTH)
        return totals[0] + smooth_abs.sum(0), totals[1] + differ / smooth_abs

    sums, slopes = lax.fori_loop(
        0, count, step, (jnp.zeros_like(misfit[0]), jnp.zeros_like(misfit))
    )
    own = jnp.sqrt(misfit * misfit + SMOOTH)
    crps = jnp.mean(own, 0) - sums / (2.0 * count * (count - 1))
    grad = misfit / own - slopes / (count - 1.0)
    grad = lax.all_to_all(grad, "ens", split_axis=0, concat_axis=2, tiled=True)[0]
    return grad, grad * (1.0 - bounded * bounded), crps


def local(members, analysis, stencils, mixing):
    _, height, breadth, channels = members.shape
    bases, span = stencils.shape[:2]
    margin = span // 2
    blocks = next(
        n for n in range(1, height + 1)
        if height % n == 0 and height // n + 2 * margin <= DEPTH // SLOTS
    )
    rows = height // blocks
    cells = height * breadth
    pair = lax.axis_size("ens") == 2
    flat = members.reshape(cells, channels)
    mine = analysis.reshape(cells, analysis.shape[2])

    odd = lax.axis_index("lat") % 2
    end = (height + margin) * SLOTS
    place = jnp.stack([
        lax.axis_index("lat") * height, odd, (1 - odd) * end, odd * end, lax.axis_index("ens")
    ]).astype(jnp.int32)

    up, down, flat = sides(flat, breadth, margin)
    left, right = ring(up, down)
    weights = call(
        load_mixing, [b16(*mixing.shape)] * 2,
        [place, pltpu.with_memory_space_constraint(mixing, pltpu.HBM)],
        [SMEM, pl.BlockSpec(memory_space=pltpu.HBM)],
        [pltpu.VMEM((4, *mixing.shape[1:]), jnp.float32), pltpu.SemaphoreType.DMA((4,))],
        size=2 * mixing.size * 4, limit=8,
    )
    if pair:
        theirs = lax.ppermute(mine, "ens", SWAP)
    band = bands(place, stencils, rows, blocks, breadth, True)
    wide, first, second = assemble(place, flat, left, right, breadth)
    first, second = swap(first, second)

    window = pltpu.VMEM(((height + 2 * margin) * SLOTS, channels), jnp.bfloat16)
    taps = [b16(bases, cells, channels)] * 2
    stencil_flops = 6 * blocks * bases * rows * breadth * DEPTH * channels
    mix_flops = 6 * cells * bases * channels * channels
    rest = channels - EDGE
    predicted1, bounded1, shigh, slow = call(
        forward_first, [f32(cells, EDGE)] * 2 + taps,
        [place, wide, first, second, *band, *weights, flat], [SMEM] + [VMEM] * 8,
        [window, window],
        flops=stencil_flops + mix_flops * EDGE // channels,
    )
    if pair:
        other1 = lax.ppermute(predicted1, "ens", SWAP)
    predicted2, bounded2 = call(
        forward_rest, [f32(cells, rest)] * 2, [shigh, slow, *weights, flat],
        flops=mix_flops * rest // channels,
    )
    back = bands(place, stencils, rows, blocks, breadth, False)
    if pair:
        other2 = lax.ppermute(predicted2, "ens", SWAP)
        (known,) = call(
            whole_analysis, [f32(cells, channels)], [place, mine, theirs],
            [SMEM, VMEM, VMEM], size=1 << 20, limit=8,
        )
        grad1, inner1 = call(
            loss_first, [f32(cells, EDGE)] * 2,
            [predicted1, other1, bounded1, known], size=1 << 20, limit=8,
        )
        side = f32(height * margin, channels)
        grad2, inner, up, down = call(
            functools.partial(loss_rest, breadth=breadth),
            [f32(cells, rest), f32(cells, channels), side, side],
            [predicted2, other2, bounded2, known, inner1], size=2 << 20, limit=8,
        )
        (crps,) = call(
            crps_kernel, [f32(*mine.shape)],
            [place, predicted1, predicted2, other1, other2, mine], [SMEM] + [VMEM] * 5,
            size=1 << 20, limit=8,
        )
    else:
        predicted = jnp.concatenate([predicted1, predicted2], 1)
        bounded = jnp.concatenate([bounded1, bounded2], 1)
        grad, inner, crps = loss_many(predicted, bounded, mine)
        grad1, grad2 = grad[:, :EDGE], grad[:, EDGE:]
        up, down, _ = sides(inner, breadth, margin)

    left, right = ring(up, down)
    wide, first, second = assemble(place, inner, left, right, breadth)
    first, second = swap(first, second)
    (result,) = call(
        backward_all, [f32(cells, channels)],
        [place, wide, first, second, *back, *weights, grad1, grad2], [SMEM] + [VMEM] * 9,
        [pltpu.VMEM(s.shape, s.dtype) for s in taps]
        + [window, window],
        flops=stencil_flops + mix_flops,
    )
    return result.reshape(members.shape), crps.reshape(analysis.shape)


def solution(mesh):
    in_specs = (P("ens", "lat", "lon", None), P("lat", "lon", "ens"), P(), P())
    out_specs = (P("ens", "lat", "lon", None), P("lat", "lon", "ens"))
    return jax.shard_map(local, mesh=mesh, in_specs=in_specs, out_specs=out_specs, check_vma=False)
```

```python
import functools

import jax
import jax.numpy as jnp
from jax import lax
from jax.experimental import pallas as pl
from jax.experimental.pallas import tpu as pltpu
from jax.sharding import PartitionSpec as P


SMOOTH = 0.01
SLOTS = 16
DEPTH = 256
EDGE = 256
SWAP = [(0, 1), (1, 0)]
VMEM = pl.BlockSpec(memory_space=pltpu.VMEM)
SMEM = pl.BlockSpec(memory_space=pltpu.SMEM)


def f32(*shape):
    return jax.ShapeDtypeStruct(shape, jnp.float32)


def b16(*shape):
    return jax.ShapeDtypeStruct(shape, jnp.bfloat16)


def split(value):
    high = value.astype(jnp.bfloat16)
    low = (value - high.astype(jnp.float32)).astype(jnp.bfloat16)
    return high, low


def product(left, right, axis):
    return lax.dot_general(
        left, right, (((1,), (axis,)), ((), ())), preferred_element_type=jnp.float32
    )


def product3(left_high, left_low, right_high, right_low, axis):
    rows = left_high.shape[0]
    both = product(jnp.concatenate([left_high, left_low], 0), right_high, axis)
    return both[:rows] + both[rows:] + product(left_high, right_low, axis)


def call(body, out_shape, operands, specs=None, scratch=(), flops=0, size=0, limit=12):
    return pl.pallas_call(
        body,
        out_shape=out_shape,
        in_specs=specs or [VMEM] * len(operands),
        out_specs=[VMEM] * len(out_shape),
        scratch_shapes=scratch,
        cost_estimate=pl.CostEstimate(flops=flops, bytes_accessed=size, transcendentals=0),
        compiler_params=pltpu.CompilerParams(vmem_limit_bytes=limit << 20),
    )(*operands)


def band_kernel(place_ref, stencils_ref, inner_ref, outer_ref, table_ref, in_ref, out_ref, *, rows, forward):
    bases, span, _, total = stencils_ref.shape
    blocks = inner_ref.shape[0]
    margin = span // 2
    breadth = outer_ref.shape[1] // (2 * bases * margin)
    first_row = place_ref[0]
    iota = lambda shape, axis: lax.broadcasted_iota(jnp.int32, shape, axis)

    table_ref[...] = jnp.zeros_like(table_ref)
    for base in range(bases):
        for tap in range(span):
            at = (base * 8 + tap) * 8
            table_ref[at : at + span, :total] = stencils_ref[base, tap]
    table = split(table_ref[...])

    group = blocks * SLOTS
    shifts = [margin] if forward else list(range(span))
    count = group * len(shifts)
    line, latitude = iota((count, table_ref.shape[1]), 0), iota((count, table_ref.shape[1]), 1)
    local_row = line % SLOTS
    shift = shifts[0] if forward else line // group
    wanted = first_row + (line % group) // SLOTS * rows + local_row + shift - margin
    picks = ((latitude == wanted) & (local_row < rows)).astype(jnp.float32).astype(jnp.bfloat16)

    width = table_ref.shape[0]
    tap_of = iota((group, width), 1) // 8 % 8
    stacked = []
    for part in table:
        picked = product(picks, part, 1)
        if forward:
            line = iota((group, width), 0)
            reach = first_row + line // SLOTS * rows + line % SLOTS + tap_of - margin
            taps = jnp.where((reach >= 0) & (reach < total), picked, 0.0)
        else:
            taps = jnp.zeros((group, width), jnp.float32)
            for tap in range(span):
                here = picked[tap * group : (tap + 1) * group]
                taps = jnp.where(tap_of == span - 1 - tap, here, taps)
        stacked += [taps[:, at : at + 128] for at in range(0, width, 128)]
    left = jnp.concatenate(stacked, 0).astype(jnp.bfloat16)
    pairs = width // 128

    source, target = iota((128, 256), 0), iota((128, 256), 1)
    slot = target % SLOTS
    column = jnp.where(
        slot < breadth,
        slot,
        jnp.where(slot < breadth + margin, slot - breadth - margin, slot - margin),
    )
    row_tap, column_tap = source // 8 % 8, source % 8
    to_row = target % 128 // SLOTS
    if not forward:
        row_tap, column_tap = span - 1 - row_tap, span - 1 - column_tap
    same = (row_tap == to_row) & (source // 64 == target // 128) & (slot < breadth + 2 * margin)
    same = same & (source % 8 < span) & (source // 8 % 8 < span)
    offset = jnp.where(same, column_tap - column, 1000)
    zeros = jnp.zeros((left.shape[0], 128), jnp.float32)
    for j in range(breadth):
        spread = (offset == margin - j).astype(jnp.float32).astype(jnp.bfloat16)
        both = product(left, spread, 0)
        for odd in range(2):
            wide = jnp.concatenate([both[:, odd * 128 : odd * 128 + 128], zeros], 1)
            wide = pltpu.roll(wide, 0, 1, stride=SLOTS, stride_axis=0)
            for part in range(2):
                for pair in range(pairs):
                    base = 2 * pair + odd
                    if base >= bases:
                        continue
                    for block in range(blocks):
                        at = ((part * pairs + pair) * blocks + block) * SLOTS
                        inner = margin if block == 0 else 0
                        outer = 0 if block == 0 else rows - margin
                        for ref, begin, count in (
                            (in_ref, inner, rows - margin), (out_ref, outer, margin),
                        ):
                            lines = pl.ds(base * count * breadth + j, count, stride=breadth)
                            for half in range(2):
                                ref[part, half, block, lines, :] = wide[
                                    at + begin : at + begin + count, half * 128 : half * 128 + 128
                                ]
    for source_ref, ref in ((in_ref, inner_ref), (out_ref, outer_ref)):
        for half in range(2):
            lanes = slice(half * 128, half * 128 + 128)
            both = jnp.concatenate([source_ref[0, half], source_ref[1, half]], 1)
            ref[:, :, lanes] = both.astype(jnp.bfloat16)


def bands(place, stencils, rows, breadth, forward):
    bases, span, _, total = stencils.shape
    margin = span // 2
    inner, outer = bases * (rows - margin) * breadth, bases * margin * breadth
    return call(
        functools.partial(band_kernel, rows=rows, forward=forward),
        [b16(2, 2 * inner, DEPTH), b16(2, 2 * outer, DEPTH)],
        [place, stencils],
        [SMEM, VMEM],
        [
            pltpu.VMEM(((bases + 1) // 2 * 128, -(-total // 128) * 128), jnp.float32),
            pltpu.VMEM((2, DEPTH // 128, 2, inner, 128), jnp.float32),
            pltpu.VMEM((2, DEPTH // 128, 2, outer, 128), jnp.float32),
        ],
        flops=10**9, size=4 << 20,
    )


def pack(place_ref, field_ref, up_ref, down_ref, first_ref, second_ref, breadth):
    height = field_ref.shape[0] // breadth
    margin = up_ref.shape[0] // height
    for row in range(height):
        at = slice(row * margin, (row + 1) * margin)
        up_ref[at, :] = field_ref[(row + 1) * breadth - margin : (row + 1) * breadth, :]
        down_ref[at, :] = field_ref[row * breadth : row * breadth + margin, :]
    low = field_ref[: margin * breadth, :]
    high = field_ref[(height - margin) * breadth :, :]
    odd = place_ref[1] == 1
    first_ref[...] = jnp.where(odd, low, high)
    second_ref[...] = jnp.where(odd, high, low)


def pack_kernel(place_ref, field_ref, up_ref, down_ref, first_ref, second_ref, kept_ref, *, breadth):
    pack(place_ref, field_ref, up_ref, down_ref, first_ref, second_ref, breadth)
    kept_ref[...] = field_ref[...]


def edges(cells, channels, breadth, margin):
    side, row = f32(cells // breadth * margin, channels), f32(margin * breadth, channels)
    return [side, side, row, row]


def corner_kernel(first_ref, second_ref, up_ref, down_ref, *, breadth, margin):
    for part, ref in enumerate((first_ref, second_ref)):
        for row in range(margin):
            at = slice((part * margin + row) * margin, (part * margin + row + 1) * margin)
            up_ref[at, :] = ref[(row + 1) * breadth - margin : (row + 1) * breadth, :]
            down_ref[at, :] = ref[row * breadth : row * breadth + margin, :]


def widen(own, left, right):
    spare = jnp.zeros((SLOTS - own.shape[0] - left.shape[0] - right.shape[0], own.shape[1]), jnp.float32)
    return jnp.concatenate([own, left, right, spare], 0)


def inner_kernel(field_ref, left_ref, right_ref, band_ref, xhigh_ref, xlow_ref, shigh_ref, slow_ref, *, breadth):
    height = field_ref.shape[0] // breadth
    margin = left_ref.shape[0] // height
    bases, cells = shigh_ref.shape[:2]
    count = cells // 2
    zeros = jnp.zeros((margin * SLOTS, field_ref.shape[1]), jnp.bfloat16)
    for ref in (xhigh_ref, xlow_ref):
        ref[: margin * SLOTS, :] = zeros
        ref[(margin + height) * SLOTS :, :] = zeros
    for row in range(height):
        here = slice(row * margin, (row + 1) * margin)
        tile = widen(field_ref[row * breadth : (row + 1) * breadth, :], left_ref[here, :], right_ref[here, :])
        at = slice((margin + row) * SLOTS, (margin + row + 1) * SLOTS)
        xhigh_ref[at, :], xlow_ref[at, :] = split(tile)
    got = []
    for block in range(2):
        window = slice(block * (height // 2) * SLOTS, block * (height // 2) * SLOTS + DEPTH)
        got.append(banded(band_ref[block], xhigh_ref[window, :], xlow_ref[window, :]))
    keep(got, shigh_ref, slow_ref, bases, count)


def banded(band, high, low):
    lines = band.shape[0] // 2
    both = product(band, high, 0)
    return both[:lines] + both[lines:] + product(band[:lines], low, 0)


def keep(got, shigh_ref, slow_ref, bases, count):
    for base in range(bases):
        at = slice(base * count, (base + 1) * count)
        shigh_ref[base], slow_ref[base] = split(jnp.concatenate([part[at] for part in got], 0))


def outer_kernel(place_ref, first_ref, second_ref, left_ref, right_ref, band_ref, xhigh_ref, xlow_ref,
                 shigh_ref, slow_ref, zhigh_ref, zlow_ref, *, breadth):
    margin = first_ref.shape[0] // breadth
    bases, cells = shigh_ref.shape[:2]
    edge = margin * SLOTS
    own = xhigh_ref.shape[0] - 2 * edge
    body = DEPTH - edge
    odd = place_ref[1] == 1
    tiles = []
    for part, ref in enumerate((first_ref, second_ref)):
        rows = []
        for row in range(margin):
            here = slice((part * margin + row) * margin, (part * margin + row + 1) * margin)
            rows.append(widen(ref[row * breadth : (row + 1) * breadth, :], left_ref[here, :], right_ref[here, :]))
        tiles.append(jnp.concatenate(rows, 0))
    low, high = jnp.where(odd, tiles[0], tiles[1]), jnp.where(odd, tiles[1], tiles[0])
    zhigh_ref[0, :edge], zlow_ref[0, :edge] = split(low)
    zhigh_ref[1, body:], zlow_ref[1, body:] = split(high)
    for ref, source_ref in ((zhigh_ref, xhigh_ref), (zlow_ref, xlow_ref)):
        ref[0, edge:] = source_ref[edge : edge + body, :]
        ref[1, :body] = source_ref[edge + own - body : edge + own, :]
    got = [banded(band_ref[block], zhigh_ref[block], zlow_ref[block]) for block in range(2)]
    keep(got, shigh_ref, slow_ref, bases, cells // 2)


def ring(up, down):
    count = lax.axis_size("lon")
    there = [(i, (i + 1) % count) for i in range(count)]
    back = [(b, a) for a, b in there]
    return lax.ppermute(up, "lon", there), lax.ppermute(down, "lon", back)


def swap(first, second):
    count = lax.axis_size("lat")

    def one(piece, lows):
        table = {i: i for i in range(count)}
        for low in lows:
            if low + 1 < count:
                table[low], table[low + 1] = low + 1, low
        return lax.ppermute(piece, "lat", sorted(table.items()))

    return (one(first, range(0, count, 2)), one(second, range(1, count, 2)))


def split_mixing(mixing_ref, high_ref, low_ref):
    for base in range(mixing_ref.shape[0]):
        high_ref[base], low_ref[base] = split(mixing_ref[base])


def contract(taps, mhigh_ref, mlow_ref, lanes, axis):
    inner_high, inner_low, outer_high, outer_low = taps
    total = None
    for base in range(mhigh_ref.shape[0]):
        high = jnp.concatenate([inner_high[base], outer_high[base]], 0)
        low = jnp.concatenate([inner_low[base], outer_low[base]], 0)
        part = product3(high, low, mhigh_ref[base, :, lanes], mlow_ref[base, :, lanes], axis)
        total = part if total is None else total + part
    edge = outer_high.shape[1] // 2
    inner = inner_high.shape[1]
    return jnp.concatenate([total[inner : inner + edge], total[:inner], total[inner + edge :]], 0)


def forward(ihigh_ref, ilow_ref, ohigh_ref, olow_ref, mhigh_ref, mlow_ref, field_ref, predicted_ref, bounded_ref, *, start):
    lanes = slice(start, start + predicted_ref.shape[1])
    total = contract((ihigh_ref, ilow_ref, ohigh_ref, olow_ref), mhigh_ref, mlow_ref, lanes, 0)
    bounded = jnp.tanh(total)
    bounded_ref[...] = bounded
    predicted_ref[...] = field_ref[:, lanes] + bounded


def backward(ihigh_ref, ilow_ref, ohigh_ref, olow_ref, mhigh_ref, mlow_ref, grad_ref, tail_ref, out_ref):
    total = contract((ihigh_ref, ilow_ref, ohigh_ref, olow_ref), mhigh_ref, mlow_ref, slice(None), 1)
    edge = grad_ref.shape[1]
    out_ref[:, :edge] = total[:, :edge] + grad_ref[...]
    out_ref[:, edge:] = total[:, edge:] + tail_ref[...]


def slope(value):
    return value * lax.rsqrt(value * value + SMOOTH)


def soft(value):
    return jnp.sqrt(value * value + SMOOTH)


def loss_first(own_ref, other_ref, bounded_ref, analysis_ref, grad_ref, inner_ref):
    analysis = analysis_ref[:, : own_ref.shape[1]]
    own = own_ref[...] - analysis
    grad = slope(own) - slope(own - (other_ref[...] - analysis))
    grad_ref[...] = grad
    inner_ref[...] = grad * (1.0 - bounded_ref[...] * bounded_ref[...])


def loss_rest(place_ref, own_ref, other_ref, bounded_ref, analysis_ref, before_ref, grad_ref, inner_ref,
              up_ref, down_ref, first_ref, second_ref, *, breadth):
    edge = before_ref.shape[1]
    analysis = analysis_ref[:, edge:]
    own = own_ref[...] - analysis
    grad = slope(own) - slope(own - (other_ref[...] - analysis))
    grad_ref[...] = grad
    inner_ref[:, :edge] = before_ref[...]
    inner_ref[:, edge:] = grad * (1.0 - bounded_ref[...] * bounded_ref[...])
    pack(place_ref, inner_ref, up_ref, down_ref, first_ref, second_ref, breadth)


def whole_analysis(place_ref, mine_ref, theirs_ref, out_ref):
    half = mine_ref.shape[1]
    first = place_ref[2] == 0
    mine, theirs = mine_ref[...], theirs_ref[...]
    out_ref[:, :half] = jnp.where(first, mine, theirs)
    out_ref[:, half:] = jnp.where(first, theirs, mine)


def crps_kernel(place_ref, own1_ref, own2_ref, other1_ref, other2_ref, mine_ref, out_ref):
    half = mine_ref.shape[1]
    edge = own1_ref.shape[1]
    for part in range(2):
        @pl.when(place_ref[2] == part)
        def _():
            low, high = part * half, (part + 1) * half
            pieces = []
            if low < edge:
                pieces.append((own1_ref, other1_ref, slice(low, min(high, edge)), 0))
            if high > edge:
                start = max(low, edge)
                pieces.append((own2_ref, other2_ref, slice(start - edge, high - edge), start - low))
            for own_ref, other_ref, lanes, at in pieces:
                here = slice(at, at + lanes.stop - lanes.start)
                mine = mine_ref[:, here]
                own = own_ref[:, lanes] - mine
                other = other_ref[:, lanes] - mine
                gap = own - other
                pair = 2.0 * (soft(gap) + jnp.sqrt(jnp.full_like(gap, SMOOTH)))
                out_ref[:, here] = 0.5 * (soft(own) + soft(other)) - pair / 4.0


def loss_many(predicted, bounded, analysis):
    grouped = lax.all_to_all(predicted[None], "ens", split_axis=2, concat_axis=0, tiled=True)
    misfit = grouped - analysis[None]
    count = misfit.shape[0]

    def step(other, totals):
        differ = misfit - lax.dynamic_index_in_dim(misfit, other, 0)
        smooth_abs = jnp.sqrt(differ * differ + SMOOTH)
        return totals[0] + smooth_abs.sum(0), totals[1] + differ / smooth_abs

    sums, slopes = lax.fori_loop(
        0, count, step, (jnp.zeros_like(misfit[0]), jnp.zeros_like(misfit))
    )
    own = jnp.sqrt(misfit * misfit + SMOOTH)
    crps = jnp.mean(own, 0) - sums / (2.0 * count * (count - 1))
    grad = misfit / own - slopes / (count - 1.0)
    grad = lax.all_to_all(grad, "ens", split_axis=0, concat_axis=2, tiled=True)[0]
    return grad, grad * (1.0 - bounded * bounded), crps


def local(members, analysis, stencils, mixing):
    _, height, breadth, channels = members.shape
    bases, span = stencils.shape[:2]
    margin = span // 2
    rows = height // 2
    assert height == 2 * rows and rows + 2 * margin <= DEPTH // SLOTS and rows >= 2 * margin
    cells = height * breadth
    pair = lax.axis_size("ens") == 2
    flat = members.reshape(cells, channels)
    mine = analysis.reshape(cells, analysis.shape[2])
    rest = channels - EDGE
    place = jnp.stack([
        lax.axis_index("lat") * height, lax.axis_index("lat") % 2, lax.axis_index("ens")
    ]).astype(jnp.int32)
    packed = edges(cells, channels, breadth, margin)
    mix_flops = 6 * cells * bases * channels * channels
    stencil_flops = 6 * bases * cells * DEPTH * channels
    inner_cells, outer_cells = cells - 2 * margin * breadth, 2 * margin * breadth

    def taps(count):
        return [b16(bases, count, channels)] * 2

    def spread(up, down, first, second, field, band):
        left, right = ring(up, down)
        first, second = swap(first, second)
        corner = f32(2 * margin * margin, channels)
        corners = call(
            functools.partial(corner_kernel, breadth=breadth, margin=margin),
            [corner, corner], [first, second], size=1 << 18, limit=4,
        )
        cleft, cright = ring(*corners)
        window = b16((height + 2 * margin) * SLOTS, channels)
        xhigh, xlow, *inner = call(
            functools.partial(inner_kernel, breadth=breadth),
            [window, window] + taps(inner_cells), [field, left, right, band[0]],
            flops=stencil_flops * 7 // 10,
        )
        depth = pltpu.VMEM((2, DEPTH, channels), jnp.bfloat16)
        outer = call(
            functools.partial(outer_kernel, breadth=breadth), taps(outer_cells),
            [place, first, second, cleft, cright, band[1], xhigh, xlow], [SMEM] + [VMEM] * 7,
            [depth, depth], flops=stencil_flops * 3 // 10,
        )
        return [*inner, *outer]

    *sent, flat = call(
        functools.partial(pack_kernel, breadth=breadth), packed + [f32(cells, channels)],
        [place, flat], [SMEM, VMEM], flops=10**10, size=1 << 20, limit=8,
    )
    band = bands(place, stencils, rows, breadth, True)
    spread0 = spread(*sent, flat, band)
    if pair:
        theirs = lax.ppermute(mine, "ens", SWAP)
    weights = call(split_mixing, [b16(*mixing.shape)] * 2, [mixing], size=mixing.size * 4)
    predicted1, bounded1 = call(
        functools.partial(forward, start=0), [f32(cells, EDGE)] * 2,
        [*spread0, *weights, flat], flops=mix_flops * EDGE // channels,
    )
    if pair:
        other1 = lax.ppermute(predicted1, "ens", SWAP)
    predicted2, bounded2 = call(
        functools.partial(forward, start=EDGE), [f32(cells, rest)] * 2,
        [*spread0, *weights, flat], flops=mix_flops * rest // channels,
    )
    back = bands(place, stencils, rows, breadth, False)
    if pair:
        other2 = lax.ppermute(predicted2, "ens", SWAP)
        (known,) = call(
            whole_analysis, [f32(cells, channels)], [place, mine, theirs],
            [SMEM, VMEM, VMEM], size=1 << 20, limit=8,
        )
        grad1, inner1 = call(
            loss_first, [f32(cells, EDGE)] * 2,
            [predicted1, other1, bounded1, known], size=1 << 20, limit=8,
        )
        grad2, inner, *sent = call(
            functools.partial(loss_rest, breadth=breadth),
            [f32(cells, rest), f32(cells, channels)] + packed,
            [place, predicted2, other2, bounded2, known, inner1], [SMEM] + [VMEM] * 5,
            size=2 << 20, limit=8,
        )
        (crps,) = call(
            crps_kernel, [f32(*mine.shape)],
            [place, predicted1, predicted2, other1, other2, mine], [SMEM] + [VMEM] * 5,
            size=1 << 20, limit=8,
        )
    else:
        predicted = jnp.concatenate([predicted1, predicted2], 1)
        bounded = jnp.concatenate([bounded1, bounded2], 1)
        grad, inner, crps = loss_many(predicted, bounded, mine)
        grad1, grad2 = grad[:, :EDGE], grad[:, EDGE:]
        *sent, inner = call(
            functools.partial(pack_kernel, breadth=breadth), packed + [f32(cells, channels)],
            [place, inner], [SMEM, VMEM], size=1 << 20, limit=8,
        )
    (result,) = call(
        backward, [f32(cells, channels)],
        [*spread(*sent, inner, back), *weights, grad1, grad2], flops=mix_flops,
    )
    return result.reshape(members.shape), crps.reshape(analysis.shape)


def solution(mesh):
    in_specs = (P("ens", "lat", "lon", None), P("lat", "lon", "ens"), P(), P())
    out_specs = (P("ens", "lat", "lon", None), P("lat", "lon", "ens"))
    return jax.shard_map(local, mesh=mesh, in_specs=in_specs, out_specs=out_specs, check_vma=False)
```

```python
import functools

import jax
import jax.numpy as jnp
from jax import lax
from jax.experimental import pallas as pl
from jax.experimental.pallas import tpu as pltpu
from jax.sharding import PartitionSpec as P


SMOOTH = 0.01
SLOTS = 16
DEPTH = 256
EDGE = 256
SWAP = [(0, 1), (1, 0)]
VMEM = pl.BlockSpec(memory_space=pltpu.VMEM)


def f32(*shape):
    return jax.ShapeDtypeStruct(shape, jnp.float32)


def b16(*shape):
    return jax.ShapeDtypeStruct(shape, jnp.bfloat16)


def split(value):
    high = value.astype(jnp.bfloat16)
    low = (value - high.astype(jnp.float32)).astype(jnp.bfloat16)
    return high, low


def product(left, right, axis):
    return lax.dot_general(
        left, right, (((1,), (axis,)), ((), ())), preferred_element_type=jnp.float32
    )


def product3(left_high, left_low, right_high, right_low, axis):
    rows = left_high.shape[0]
    both = product(jnp.concatenate([left_high, left_low], 0), right_high, axis)
    return both[:rows] + both[rows:] + product(left_high, right_low, axis)


def call(body, out_shape, operands, specs=None, scratch=(), flops=0, size=0, limit=12):
    return pl.pallas_call(
        body,
        out_shape=out_shape,
        in_specs=specs or [VMEM] * len(operands),
        out_specs=[VMEM] * len(out_shape),
        scratch_shapes=scratch,
        cost_estimate=pl.CostEstimate(flops=flops, bytes_accessed=size, transcendentals=0),
        compiler_params=pltpu.CompilerParams(vmem_limit_bytes=limit << 20),
    )(*operands)


def band_kernel(stencils_ref, inner_ref, outer_ref, table_ref, in_ref, out_ref, *, rows, forward):
    bases, span, _, total = stencils_ref.shape
    blocks = inner_ref.shape[0]
    margin = span // 2
    breadth = outer_ref.shape[1] // (2 * bases * margin)
    first_row = lax.axis_index("lat") * (2 * rows)
    iota = lambda shape, axis: lax.broadcasted_iota(jnp.int32, shape, axis)

    table_ref[...] = jnp.zeros_like(table_ref)
    for base in range(bases):
        for tap in range(span):
            at = (base * 8 + tap) * 8
            table_ref[at : at + span, :total] = stencils_ref[base, tap]
    table = split(table_ref[...])

    group = blocks * SLOTS
    shifts = [margin] if forward else list(range(span))
    count = group * len(shifts)
    line, latitude = iota((count, table_ref.shape[1]), 0), iota((count, table_ref.shape[1]), 1)
    local_row = line % SLOTS
    shift = shifts[0] if forward else line // group
    wanted = first_row + (line % group) // SLOTS * rows + local_row + shift - margin
    picks = ((latitude == wanted) & (local_row < rows)).astype(jnp.float32).astype(jnp.bfloat16)

    width = table_ref.shape[0]
    tap_of = iota((group, width), 1) // 8 % 8
    stacked = []
    for part in table:
        picked = product(picks, part, 1)
        if forward:
            line = iota((group, width), 0)
            reach = first_row + line // SLOTS * rows + line % SLOTS + tap_of - margin
            taps = jnp.where((reach >= 0) & (reach < total), picked, 0.0)
        else:
            taps = jnp.zeros((group, width), jnp.float32)
            for tap in range(span):
                here = picked[tap * group : (tap + 1) * group]
                taps = jnp.where(tap_of == span - 1 - tap, here, taps)
        stacked += [taps[:, at : at + 128] for at in range(0, width, 128)]
    left = jnp.concatenate(stacked, 0).astype(jnp.bfloat16)
    pairs = width // 128

    source, target = iota((128, 256), 0), iota((128, 256), 1)
    slot = target % SLOTS
    column = jnp.where(
        slot < breadth,
        slot,
        jnp.where(slot < breadth + margin, slot - breadth - margin, slot - margin),
    )
    row_tap, column_tap = source // 8 % 8, source % 8
    to_row = target % 128 // SLOTS
    if not forward:
        row_tap, column_tap = span - 1 - row_tap, span - 1 - column_tap
    same = (row_tap == to_row) & (source // 64 == target // 128) & (slot < breadth + 2 * margin)
    same = same & (source % 8 < span) & (source // 8 % 8 < span)
    offset = jnp.where(same, column_tap - column, 1000)
    zeros = jnp.zeros((left.shape[0], 128), jnp.float32)
    for j in range(breadth):
        spread = (offset == margin - j).astype(jnp.float32).astype(jnp.bfloat16)
        both = product(left, spread, 0)
        for odd in range(2):
            wide = jnp.concatenate([both[:, odd * 128 : odd * 128 + 128], zeros], 1)
            wide = pltpu.roll(wide, 0, 1, stride=SLOTS, stride_axis=0)
            for part in range(2):
                for pair in range(pairs):
                    base = 2 * pair + odd
                    if base >= bases:
                        continue
                    for block in range(blocks):
                        at = ((part * pairs + pair) * blocks + block) * SLOTS
                        inner = margin if block == 0 else 0
                        outer = 0 if block == 0 else rows - margin
                        for ref, begin, count in (
                            (in_ref, inner, rows - margin), (out_ref, outer, margin),
                        ):
                            lines = pl.ds(base * count * breadth + j, count, stride=breadth)
                            for half in range(2):
                                ref[part, half, block, lines, :] = wide[
                                    at + begin : at + begin + count, half * 128 : half * 128 + 128
                                ]
    for source_ref, ref in ((in_ref, inner_ref), (out_ref, outer_ref)):
        for half in range(2):
            lanes = slice(half * 128, half * 128 + 128)
            both = jnp.concatenate([source_ref[0, half], source_ref[1, half]], 1)
            ref[:, :, lanes] = both.astype(jnp.bfloat16)


def bands(stencils, rows, breadth, forward):
    bases, span, _, total = stencils.shape
    margin = span // 2
    inner, outer = bases * (rows - margin) * breadth, bases * margin * breadth
    return call(
        functools.partial(band_kernel, rows=rows, forward=forward),
        [b16(2, 2 * inner, DEPTH), b16(2, 2 * outer, DEPTH)],
        [stencils],
        scratch=[
            pltpu.VMEM(((bases + 1) // 2 * 128, -(-total // 128) * 128), jnp.float32),
            pltpu.VMEM((2, DEPTH // 128, 2, inner, 128), jnp.float32),
            pltpu.VMEM((2, DEPTH // 128, 2, outer, 128), jnp.float32),
        ],
        flops=10**9, size=4 << 20,
    )


def pack(field_ref, up_ref, down_ref, first_ref, second_ref, breadth):
    height = field_ref.shape[0] // breadth
    margin = up_ref.shape[0] // height
    for row in range(height):
        at = slice(row * margin, (row + 1) * margin)
        up_ref[at, :] = field_ref[(row + 1) * breadth - margin : (row + 1) * breadth, :]
        down_ref[at, :] = field_ref[row * breadth : row * breadth + margin, :]
    low = field_ref[: margin * breadth, :]
    high = field_ref[(height - margin) * breadth :, :]
    odd = lax.axis_index("lat") % 2 == 1
    first_ref[...] = jnp.where(odd, low, high)
    second_ref[...] = jnp.where(odd, high, low)


def pack_kernel(field_ref, up_ref, down_ref, first_ref, second_ref, kept_ref, *, breadth):
    pack(field_ref, up_ref, down_ref, first_ref, second_ref, breadth)
    kept_ref[...] = field_ref[...]


def edges(cells, channels, breadth, margin):
    side, row = f32(cells // breadth * margin, channels), f32(margin * breadth, channels)
    return [side, side, row, row]


def corner_kernel(first_ref, second_ref, up_ref, down_ref, *, breadth, margin):
    for part, ref in enumerate((first_ref, second_ref)):
        for row in range(margin):
            at = slice((part * margin + row) * margin, (part * margin + row + 1) * margin)
            up_ref[at, :] = ref[(row + 1) * breadth - margin : (row + 1) * breadth, :]
            down_ref[at, :] = ref[row * breadth : row * breadth + margin, :]


def widen(own, left, right):
    spare = jnp.zeros((SLOTS - own.shape[0] - left.shape[0] - right.shape[0], own.shape[1]), jnp.float32)
    return jnp.concatenate([own, left, right, spare], 0)


def inner_kernel(field_ref, left_ref, right_ref, band_ref, xhigh_ref, xlow_ref, shigh_ref, slow_ref, *, breadth):
    height = field_ref.shape[0] // breadth
    margin = left_ref.shape[0] // height
    bases, cells = shigh_ref.shape[:2]
    count = cells // 2
    zeros = jnp.zeros((margin * SLOTS, field_ref.shape[1]), jnp.bfloat16)
    for ref in (xhigh_ref, xlow_ref):
        ref[: margin * SLOTS, :] = zeros
        ref[(margin + height) * SLOTS :, :] = zeros
    for row in range(height):
        here = slice(row * margin, (row + 1) * margin)
        tile = widen(field_ref[row * breadth : (row + 1) * breadth, :], left_ref[here, :], right_ref[here, :])
        at = slice((margin + row) * SLOTS, (margin + row + 1) * SLOTS)
        xhigh_ref[at, :], xlow_ref[at, :] = split(tile)
    got = []
    for block in range(2):
        window = slice(block * (height // 2) * SLOTS, block * (height // 2) * SLOTS + DEPTH)
        got.append(banded(band_ref[block], xhigh_ref[window, :], xlow_ref[window, :]))
    keep(got, shigh_ref, slow_ref, bases, count)


def banded(band, high, low):
    lines = band.shape[0] // 2
    both = product(band, high, 0)
    return both[:lines] + both[lines:] + product(band[:lines], low, 0)


def keep(got, shigh_ref, slow_ref, bases, count):
    for base in range(bases):
        at = slice(base * count, (base + 1) * count)
        shigh_ref[base], slow_ref[base] = split(jnp.concatenate([part[at] for part in got], 0))


def outer_kernel(first_ref, second_ref, left_ref, right_ref, band_ref, xhigh_ref, xlow_ref,
                 shigh_ref, slow_ref, zhigh_ref, zlow_ref, *, breadth):
    margin = first_ref.shape[0] // breadth
    bases, cells = shigh_ref.shape[:2]
    edge = margin * SLOTS
    own = xhigh_ref.shape[0] - 2 * edge
    body = DEPTH - edge
    odd = lax.axis_index("lat") % 2 == 1
    tiles = []
    for part, ref in enumerate((first_ref, second_ref)):
        rows = []
        for row in range(margin):
            here = slice((part * margin + row) * margin, (part * margin + row + 1) * margin)
            rows.append(widen(ref[row * breadth : (row + 1) * breadth, :], left_ref[here, :], right_ref[here, :]))
        tiles.append(jnp.concatenate(rows, 0))
    low, high = jnp.where(odd, tiles[0], tiles[1]), jnp.where(odd, tiles[1], tiles[0])
    zhigh_ref[0, :edge], zlow_ref[0, :edge] = split(low)
    zhigh_ref[1, body:], zlow_ref[1, body:] = split(high)
    for ref, source_ref in ((zhigh_ref, xhigh_ref), (zlow_ref, xlow_ref)):
        ref[0, edge:] = source_ref[edge : edge + body, :]
        ref[1, :body] = source_ref[edge + own - body : edge + own, :]
    got = [banded(band_ref[block], zhigh_ref[block], zlow_ref[block]) for block in range(2)]
    keep(got, shigh_ref, slow_ref, bases, cells // 2)


def ring(up, down):
    count = lax.axis_size("lon")
    there = [(i, (i + 1) % count) for i in range(count)]
    back = [(b, a) for a, b in there]
    return lax.ppermute(up, "lon", there), lax.ppermute(down, "lon", back)


def swap(first, second):
    count = lax.axis_size("lat")

    def one(piece, lows):
        table = {i: i for i in range(count)}
        for low in lows:
            if low + 1 < count:
                table[low], table[low + 1] = low + 1, low
        return lax.ppermute(piece, "lat", sorted(table.items()))

    return (one(first, range(0, count, 2)), one(second, range(1, count, 2)))


def split_mixing(mixing_ref, high_ref, low_ref):
    for base in range(mixing_ref.shape[0]):
        high_ref[base], low_ref[base] = split(mixing_ref[base])


def contract(taps, mhigh_ref, mlow_ref, lanes, axis):
    inner_high, inner_low, outer_high, outer_low = taps
    total = None
    for base in range(mhigh_ref.shape[0]):
        high = jnp.concatenate([inner_high[base], outer_high[base]], 0)
        low = jnp.concatenate([inner_low[base], outer_low[base]], 0)
        part = product3(high, low, mhigh_ref[base, :, lanes], mlow_ref[base, :, lanes], axis)
        total = part if total is None else total + part
    edge = outer_high.shape[1] // 2
    inner = inner_high.shape[1]
    return jnp.concatenate([total[inner : inner + edge], total[:inner], total[inner + edge :]], 0)


def forward(ihigh_ref, ilow_ref, ohigh_ref, olow_ref, mhigh_ref, mlow_ref, field_ref, predicted_ref, bounded_ref, *, start):
    lanes = slice(start, start + predicted_ref.shape[1])
    total = contract((ihigh_ref, ilow_ref, ohigh_ref, olow_ref), mhigh_ref, mlow_ref, lanes, 0)
    bounded = jnp.tanh(total)
    bounded_ref[...] = bounded
    predicted_ref[...] = field_ref[:, lanes] + bounded


def backward(ihigh_ref, ilow_ref, ohigh_ref, olow_ref, mhigh_ref, mlow_ref, grad_ref, tail_ref, out_ref):
    total = contract((ihigh_ref, ilow_ref, ohigh_ref, olow_ref), mhigh_ref, mlow_ref, slice(None), 1)
    edge = grad_ref.shape[1]
    out_ref[:, :edge] = total[:, :edge] + grad_ref[...]
    out_ref[:, edge:] = total[:, edge:] + tail_ref[...]


def slope(value):
    return value * lax.rsqrt(value * value + SMOOTH)


def soft(value):
    return jnp.sqrt(value * value + SMOOTH)


def loss_first(own_ref, other_ref, bounded_ref, analysis_ref, grad_ref, inner_ref):
    analysis = analysis_ref[:, : own_ref.shape[1]]
    own = own_ref[...] - analysis
    grad = slope(own) - slope(own - (other_ref[...] - analysis))
    grad_ref[...] = grad
    inner_ref[...] = grad * (1.0 - bounded_ref[...] * bounded_ref[...])


def loss_rest(own_ref, other_ref, bounded_ref, analysis_ref, before_ref, grad_ref, inner_ref,
              up_ref, down_ref, first_ref, second_ref, *, breadth):
    edge = before_ref.shape[1]
    analysis = analysis_ref[:, edge:]
    own = own_ref[...] - analysis
    grad = slope(own) - slope(own - (other_ref[...] - analysis))
    grad_ref[...] = grad
    inner_ref[:, :edge] = before_ref[...]
    inner_ref[:, edge:] = grad * (1.0 - bounded_ref[...] * bounded_ref[...])
    pack(inner_ref, up_ref, down_ref, first_ref, second_ref, breadth)


def whole_analysis(mine_ref, theirs_ref, out_ref):
    half = mine_ref.shape[1]
    first = lax.axis_index("ens") == 0
    mine, theirs = mine_ref[...], theirs_ref[...]
    out_ref[:, :half] = jnp.where(first, mine, theirs)
    out_ref[:, half:] = jnp.where(first, theirs, mine)


def crps_kernel(own1_ref, own2_ref, other1_ref, other2_ref, mine_ref, out_ref):
    half = mine_ref.shape[1]
    edge = own1_ref.shape[1]
    for part in range(2):
        @pl.when(lax.axis_index("ens") == part)
        def _():
            low, high = part * half, (part + 1) * half
            pieces = []
            if low < edge:
                pieces.append((own1_ref, other1_ref, slice(low, min(high, edge)), 0))
            if high > edge:
                start = max(low, edge)
                pieces.append((own2_ref, other2_ref, slice(start - edge, high - edge), start - low))
            for own_ref, other_ref, lanes, at in pieces:
                here = slice(at, at + lanes.stop - lanes.start)
                mine = mine_ref[:, here]
                own = own_ref[:, lanes] - mine
                other = other_ref[:, lanes] - mine
                gap = own - other
                pair = 2.0 * (soft(gap) + jnp.sqrt(jnp.full_like(gap, SMOOTH)))
                out_ref[:, here] = 0.5 * (soft(own) + soft(other)) - pair / 4.0


def loss_many(predicted, bounded, analysis):
    grouped = lax.all_to_all(predicted[None], "ens", split_axis=2, concat_axis=0, tiled=True)
    misfit = grouped - analysis[None]
    count = misfit.shape[0]

    def step(other, totals):
        differ = misfit - lax.dynamic_index_in_dim(misfit, other, 0)
        smooth_abs = jnp.sqrt(differ * differ + SMOOTH)
        return totals[0] + smooth_abs.sum(0), totals[1] + differ / smooth_abs

    sums, slopes = lax.fori_loop(
        0, count, step, (jnp.zeros_like(misfit[0]), jnp.zeros_like(misfit))
    )
    own = jnp.sqrt(misfit * misfit + SMOOTH)
    crps = jnp.mean(own, 0) - sums / (2.0 * count * (count - 1))
    grad = misfit / own - slopes / (count - 1.0)
    grad = lax.all_to_all(grad, "ens", split_axis=0, concat_axis=2, tiled=True)[0]
    return grad, grad * (1.0 - bounded * bounded), crps


def local(members, analysis, stencils, mixing):
    _, height, breadth, channels = members.shape
    bases, span = stencils.shape[:2]
    margin = span // 2
    rows = height // 2
    assert height == 2 * rows and rows + 2 * margin <= DEPTH // SLOTS and rows >= 2 * margin
    cells = height * breadth
    pair = lax.axis_size("ens") == 2
    flat = members.reshape(cells, channels)
    mine = analysis.reshape(cells, analysis.shape[2])
    rest = channels - EDGE
    packed = edges(cells, channels, breadth, margin)
    mix_flops = 6 * cells * bases * channels * channels
    stencil_flops = 6 * bases * cells * DEPTH * channels
    inner_cells, outer_cells = cells - 2 * margin * breadth, 2 * margin * breadth

    def taps(count):
        return [b16(bases, count, channels)] * 2

    def spread(up, down, first, second, field, band):
        left, right = ring(up, down)
        first, second = swap(first, second)
        corner = f32(2 * margin * margin, channels)
        corners = call(
            functools.partial(corner_kernel, breadth=breadth, margin=margin),
            [corner, corner], [first, second], size=1 << 18, limit=4,
        )
        cleft, cright = ring(*corners)
        window = b16((height + 2 * margin) * SLOTS, channels)
        xhigh, xlow, *inner = call(
            functools.partial(inner_kernel, breadth=breadth),
            [window, window] + taps(inner_cells), [field, left, right, band[0]],
            flops=stencil_flops * 7 // 10,
        )
        depth = pltpu.VMEM((2, DEPTH, channels), jnp.bfloat16)
        outer = call(
            functools.partial(outer_kernel, breadth=breadth), taps(outer_cells),
            [first, second, cleft, cright, band[1], xhigh, xlow],
            scratch=[depth, depth], flops=stencil_flops * 3 // 10,
        )
        return [*inner, *outer]

    *sent, flat = call(
        functools.partial(pack_kernel, breadth=breadth), packed + [f32(cells, channels)],
        [flat], flops=10**10, size=1 << 20, limit=8,
    )
    band = bands(stencils, rows, breadth, True)
    spread0 = spread(*sent, flat, band)
    if pair:
        theirs = lax.ppermute(mine, "ens", SWAP)
    weights = call(split_mixing, [b16(*mixing.shape)] * 2, [mixing], size=mixing.size * 4)
    predicted1, bounded1 = call(
        functools.partial(forward, start=0), [f32(cells, EDGE)] * 2,
        [*spread0, *weights, flat], flops=mix_flops * EDGE // channels,
    )
    if pair:
        other1 = lax.ppermute(predicted1, "ens", SWAP)
    predicted2, bounded2 = call(
        functools.partial(forward, start=EDGE), [f32(cells, rest)] * 2,
        [*spread0, *weights, flat], flops=mix_flops * rest // channels,
    )
    back = bands(stencils, rows, breadth, False)
    if pair:
        other2 = lax.ppermute(predicted2, "ens", SWAP)
        (known,) = call(
            whole_analysis, [f32(cells, channels)], [mine, theirs],
            size=1 << 20, limit=8,
        )
        grad1, inner1 = call(
            loss_first, [f32(cells, EDGE)] * 2,
            [predicted1, other1, bounded1, known], size=1 << 20, limit=8,
        )
        grad2, inner, *sent = call(
            functools.partial(loss_rest, breadth=breadth),
            [f32(cells, rest), f32(cells, channels)] + packed,
            [predicted2, other2, bounded2, known, inner1],
            size=2 << 20, limit=8,
        )
        (crps,) = call(
            crps_kernel, [f32(*mine.shape)],
            [predicted1, predicted2, other1, other2, mine],
            size=1 << 20, limit=8,
        )
    else:
        predicted = jnp.concatenate([predicted1, predicted2], 1)
        bounded = jnp.concatenate([bounded1, bounded2], 1)
        grad, inner, crps = loss_many(predicted, bounded, mine)
        grad1, grad2 = grad[:, :EDGE], grad[:, EDGE:]
        *sent, inner = call(
            functools.partial(pack_kernel, breadth=breadth), packed + [f32(cells, channels)],
            [inner], size=1 << 20, limit=8,
        )
    (result,) = call(
        backward, [f32(cells, channels)],
        [*spread(*sent, inner, back), *weights, grad1, grad2], flops=mix_flops,
    )
    return result.reshape(members.shape), crps.reshape(analysis.shape)


def solution(mesh):
    in_specs = (P("ens", "lat", "lon", None), P("lat", "lon", "ens"), P(), P())
    out_specs = (P("ens", "lat", "lon", None), P("lat", "lon", "ens"))
    return jax.shard_map(local, mesh=mesh, in_specs=in_specs, out_specs=out_specs, check_vma=False)
```

```python
import functools

import jax
import jax.numpy as jnp
from jax import lax
from jax.experimental import pallas as pl
from jax.experimental.pallas import tpu as pltpu
from jax.sharding import PartitionSpec as P


SMOOTH = 0.01
SLOTS = 16
DEPTH = 256
EDGE = 256
SWAP = [(0, 1), (1, 0)]
VMEM = pl.BlockSpec(memory_space=pltpu.VMEM)


def f32(*shape):
    return jax.ShapeDtypeStruct(shape, jnp.float32)


def b16(*shape):
    return jax.ShapeDtypeStruct(shape, jnp.bfloat16)


def split(value):
    high = value.astype(jnp.bfloat16)
    low = (value - high.astype(jnp.float32)).astype(jnp.bfloat16)
    return high, low


def product(left, right, axis):
    return lax.dot_general(
        left, right, (((1,), (axis,)), ((), ())), preferred_element_type=jnp.float32
    )


def product3(left_high, left_low, right_high, right_low, axis):
    rows = left_high.shape[0]
    both = product(jnp.concatenate([left_high, left_low], 0), right_high, axis)
    return both[:rows] + both[rows:] + product(left_high, right_low, axis)


def call(body, out_shape, operands, specs=None, scratch=(), flops=0, size=0, limit=12):
    return pl.pallas_call(
        body,
        out_shape=out_shape,
        in_specs=specs or [VMEM] * len(operands),
        out_specs=[VMEM] * len(out_shape),
        scratch_shapes=scratch,
        cost_estimate=pl.CostEstimate(flops=flops, bytes_accessed=size, transcendentals=0),
        compiler_params=pltpu.CompilerParams(vmem_limit_bytes=limit << 20),
    )(*operands)


def band_kernel(stencils_ref, inner_ref, outer_ref, table_ref, in_ref, out_ref, *, rows, forward):
    bases, span, _, total = stencils_ref.shape
    blocks = inner_ref.shape[0]
    margin = span // 2
    breadth = outer_ref.shape[1] // (2 * bases * margin)
    first_row = lax.axis_index("lat") * (2 * rows)
    iota = lambda shape, axis: lax.broadcasted_iota(jnp.int32, shape, axis)

    table_ref[...] = jnp.zeros_like(table_ref)
    for base in range(bases):
        for tap in range(span):
            at = (base * 8 + tap) * 8
            table_ref[at : at + span, :total] = stencils_ref[base, tap]
    table = split(table_ref[...])

    group = blocks * SLOTS
    shifts = [margin] if forward else list(range(span))
    count = group * len(shifts)
    line, latitude = iota((count, table_ref.shape[1]), 0), iota((count, table_ref.shape[1]), 1)
    local_row = line % SLOTS
    shift = shifts[0] if forward else line // group
    wanted = first_row + (line % group) // SLOTS * rows + local_row + shift - margin
    picks = ((latitude == wanted) & (local_row < rows)).astype(jnp.float32).astype(jnp.bfloat16)

    width = table_ref.shape[0]
    tap_of = iota((group, width), 1) // 8 % 8
    stacked = []
    for part in table:
        picked = product(picks, part, 1)
        if forward:
            line = iota((group, width), 0)
            reach = first_row + line // SLOTS * rows + line % SLOTS + tap_of - margin
            taps = jnp.where((reach >= 0) & (reach < total), picked, 0.0)
        else:
            taps = jnp.zeros((group, width), jnp.float32)
            for tap in range(span):
                here = picked[tap * group : (tap + 1) * group]
                taps = jnp.where(tap_of == span - 1 - tap, here, taps)
        stacked += [taps[:, at : at + 128] for at in range(0, width, 128)]
    left = jnp.concatenate(stacked, 0).astype(jnp.bfloat16)
    pairs = width // 128

    source, target = iota((128, 256), 0), iota((128, 256), 1)
    slot = target % SLOTS
    column = jnp.where(
        slot < breadth,
        slot,
        jnp.where(slot < breadth + margin, slot - breadth - margin, slot - margin),
    )
    row_tap, column_tap = source // 8 % 8, source % 8
    to_row = target % 128 // SLOTS
    if not forward:
        row_tap, column_tap = span - 1 - row_tap, span - 1 - column_tap
    same = (row_tap == to_row) & (source // 64 == target // 128) & (slot < breadth + 2 * margin)
    same = same & (source % 8 < span) & (source // 8 % 8 < span)
    offset = jnp.where(same, column_tap - column, 1000)
    zeros = jnp.zeros((left.shape[0], 128), jnp.float32)
    for j in range(breadth):
        spread = (offset == margin - j).astype(jnp.float32).astype(jnp.bfloat16)
        both = product(left, spread, 0)
        for odd in range(2):
            wide = jnp.concatenate([both[:, odd * 128 : odd * 128 + 128], zeros], 1)
            wide = pltpu.roll(wide, 0, 1, stride=SLOTS, stride_axis=0)
            for part in range(2):
                for pair in range(pairs):
                    base = 2 * pair + odd
                    if base >= bases:
                        continue
                    for block in range(blocks):
                        at = ((part * pairs + pair) * blocks + block) * SLOTS
                        inner = margin if block == 0 else 0
                        outer = 0 if block == 0 else rows - margin
                        for ref, begin, count in (
                            (in_ref, inner, rows - margin), (out_ref, outer, margin),
                        ):
                            lines = pl.ds(base * count * breadth + j, count, stride=breadth)
                            for half in range(2):
                                ref[part, half, block, lines, :] = wide[
                                    at + begin : at + begin + count, half * 128 : half * 128 + 128
                                ]
    for source_ref, ref in ((in_ref, inner_ref), (out_ref, outer_ref)):
        for half in range(2):
            lanes = slice(half * 128, half * 128 + 128)
            both = jnp.concatenate([source_ref[0, half], source_ref[1, half]], 1)
            ref[:, :, lanes] = both.astype(jnp.bfloat16)


def bands(stencils, rows, breadth, forward):
    bases, span, _, total = stencils.shape
    margin = span // 2
    inner, outer = bases * (rows - margin) * breadth, bases * margin * breadth
    return call(
        functools.partial(band_kernel, rows=rows, forward=forward),
        [b16(2, 2 * inner, DEPTH), b16(2, 2 * outer, DEPTH)],
        [stencils],
        scratch=[
            pltpu.VMEM(((bases + 1) // 2 * 128, -(-total // 128) * 128), jnp.float32),
            pltpu.VMEM((2, DEPTH // 128, 2, inner, 128), jnp.float32),
            pltpu.VMEM((2, DEPTH // 128, 2, outer, 128), jnp.float32),
        ],
        flops=10**9, size=4 << 20,
    )


def odd_place(axis):
    return lax.axis_index(axis) % 2 == 1


def facing(tile, margin, odd):
    low, high = tile[:margin], tile[tile.shape[0] - margin :]
    return jnp.where(odd, high, low), jnp.where(odd, low, high)


def pack(field_ref, cross_ref, chip_ref, first_ref, second_ref, breadth):
    height = field_ref.shape[0] // breadth
    margin = cross_ref.shape[0] // height
    odd = odd_place("lon")
    for row in range(height):
        at = slice(row * margin, (row + 1) * margin)
        tile = field_ref[row * breadth : (row + 1) * breadth, :]
        cross_ref[at, :], chip_ref[at, :] = facing(tile, margin, odd)
    low = field_ref[: margin * breadth, :]
    high = field_ref[(height - margin) * breadth :, :]
    odd = odd_place("lat")
    first_ref[...] = jnp.where(odd, low, high)
    second_ref[...] = jnp.where(odd, high, low)


def pack_kernel(field_ref, cross_ref, chip_ref, first_ref, second_ref, kept_ref, *, breadth):
    pack(field_ref, cross_ref, chip_ref, first_ref, second_ref, breadth)
    kept_ref[...] = field_ref[...]


def edges(cells, channels, breadth, margin):
    side, row = f32(cells // breadth * margin, channels), f32(margin * breadth, channels)
    return [side, side, row, row]


def corner_kernel(first_ref, second_ref, cross_ref, chip_ref, *, breadth, margin):
    odd = odd_place("lon")
    for part, ref in enumerate((first_ref, second_ref)):
        for row in range(margin):
            at = slice((part * margin + row) * margin, (part * margin + row + 1) * margin)
            tile = ref[row * breadth : (row + 1) * breadth, :]
            cross_ref[at, :], chip_ref[at, :] = facing(tile, margin, odd)


def sides_of(cross_ref, chip_ref):
    odd = odd_place("lon")
    cross, chip = cross_ref[...], chip_ref[...]
    return jnp.where(odd, chip, cross), jnp.where(odd, cross, chip)


def widen(own, left, right):
    spare = jnp.zeros((SLOTS - own.shape[0] - left.shape[0] - right.shape[0], own.shape[1]), jnp.float32)
    return jnp.concatenate([own, left, right, spare], 0)


def inner_kernel(field_ref, cross_ref, chip_ref, band_ref, xhigh_ref, xlow_ref, shigh_ref, slow_ref, *, breadth):
    height = field_ref.shape[0] // breadth
    margin = cross_ref.shape[0] // height
    left, right = sides_of(cross_ref, chip_ref)
    bases, cells = shigh_ref.shape[:2]
    count = cells // 2
    zeros = jnp.zeros((margin * SLOTS, field_ref.shape[1]), jnp.bfloat16)
    for ref in (xhigh_ref, xlow_ref):
        ref[: margin * SLOTS, :] = zeros
        ref[(margin + height) * SLOTS :, :] = zeros
    for row in range(height):
        here = slice(row * margin, (row + 1) * margin)
        tile = widen(field_ref[row * breadth : (row + 1) * breadth, :], left[here], right[here])
        at = slice((margin + row) * SLOTS, (margin + row + 1) * SLOTS)
        xhigh_ref[at, :], xlow_ref[at, :] = split(tile)
    got = []
    for block in range(2):
        window = slice(block * (height // 2) * SLOTS, block * (height // 2) * SLOTS + DEPTH)
        got.append(banded(band_ref[block], xhigh_ref[window, :], xlow_ref[window, :]))
    keep(got, shigh_ref, slow_ref, bases, count)


def banded(band, high, low):
    lines = band.shape[0] // 2
    both = product(band, high, 0)
    return both[:lines] + both[lines:] + product(band[:lines], low, 0)


def keep(got, shigh_ref, slow_ref, bases, count):
    for base in range(bases):
        at = slice(base * count, (base + 1) * count)
        shigh_ref[base], slow_ref[base] = split(jnp.concatenate([part[at] for part in got], 0))


def outer_kernel(first_ref, second_ref, cross_ref, chip_ref, band_ref, xhigh_ref, xlow_ref,
                 shigh_ref, slow_ref, zhigh_ref, zlow_ref, *, breadth):
    margin = first_ref.shape[0] // breadth
    bases, cells = shigh_ref.shape[:2]
    edge = margin * SLOTS
    own = xhigh_ref.shape[0] - 2 * edge
    body = DEPTH - edge
    left, right = sides_of(cross_ref, chip_ref)
    odd = odd_place("lat")
    tiles = []
    for part, ref in enumerate((first_ref, second_ref)):
        rows = []
        for row in range(margin):
            here = slice((part * margin + row) * margin, (part * margin + row + 1) * margin)
            rows.append(widen(ref[row * breadth : (row + 1) * breadth, :], left[here], right[here]))
        tiles.append(jnp.concatenate(rows, 0))
    low, high = jnp.where(odd, tiles[0], tiles[1]), jnp.where(odd, tiles[1], tiles[0])
    zhigh_ref[0, :edge], zlow_ref[0, :edge] = split(low)
    zhigh_ref[1, body:], zlow_ref[1, body:] = split(high)
    for ref, source_ref in ((zhigh_ref, xhigh_ref), (zlow_ref, xlow_ref)):
        ref[0, edge:] = source_ref[edge : edge + body, :]
        ref[1, :body] = source_ref[edge + own - body : edge + own, :]
    got = [banded(band_ref[block], zhigh_ref[block], zlow_ref[block]) for block in range(2)]
    keep(got, shigh_ref, slow_ref, bases, cells // 2)


def swap_lon(cross, chip):
    count = lax.axis_size("lon")
    assert count % 2 == 0
    near = [(i, i ^ 1) for i in range(count)]
    far = [(i, (i + 1 if i % 2 else i - 1) % count) for i in range(count)]
    return lax.ppermute(cross, "lon", far), lax.ppermute(chip, "lon", near)


def swap(first, second):
    count = lax.axis_size("lat")

    def one(piece, lows):
        table = {i: i for i in range(count)}
        for low in lows:
            if low + 1 < count:
                table[low], table[low + 1] = low + 1, low
        return lax.ppermute(piece, "lat", sorted(table.items()))

    return (one(first, range(0, count, 2)), one(second, range(1, count, 2)))


def split_mixing(mixing_ref, high_ref, low_ref):
    for base in range(mixing_ref.shape[0]):
        high_ref[base], low_ref[base] = split(mixing_ref[base])


def contract(taps, mhigh_ref, mlow_ref, lanes, axis):
    inner_high, inner_low, outer_high, outer_low = taps
    total = None
    for base in range(mhigh_ref.shape[0]):
        high = jnp.concatenate([inner_high[base], outer_high[base]], 0)
        low = jnp.concatenate([inner_low[base], outer_low[base]], 0)
        part = product3(high, low, mhigh_ref[base, :, lanes], mlow_ref[base, :, lanes], axis)
        total = part if total is None else total + part
    edge = outer_high.shape[1] // 2
    inner = inner_high.shape[1]
    return jnp.concatenate([total[inner : inner + edge], total[:inner], total[inner + edge :]], 0)


def forward(ihigh_ref, ilow_ref, ohigh_ref, olow_ref, mhigh_ref, mlow_ref, field_ref, predicted_ref, bounded_ref, *, start):
    lanes = slice(start, start + predicted_ref.shape[1])
    total = contract((ihigh_ref, ilow_ref, ohigh_ref, olow_ref), mhigh_ref, mlow_ref, lanes, 0)
    bounded = jnp.tanh(total)
    bounded_ref[...] = bounded
    predicted_ref[...] = field_ref[:, lanes] + bounded


def backward(ihigh_ref, ilow_ref, ohigh_ref, olow_ref, mhigh_ref, mlow_ref, grad_ref, tail_ref, out_ref):
    total = contract((ihigh_ref, ilow_ref, ohigh_ref, olow_ref), mhigh_ref, mlow_ref, slice(None), 1)
    edge = grad_ref.shape[1]
    out_ref[:, :edge] = total[:, :edge] + grad_ref[...]
    out_ref[:, edge:] = total[:, edge:] + tail_ref[...]


def slope(value):
    return value * lax.rsqrt(value * value + SMOOTH)


def soft(value):
    return jnp.sqrt(value * value + SMOOTH)


def loss_first(own_ref, other_ref, bounded_ref, analysis_ref, grad_ref, inner_ref):
    analysis = analysis_ref[:, : own_ref.shape[1]]
    own = own_ref[...] - analysis
    grad = slope(own) - slope(own - (other_ref[...] - analysis))
    grad_ref[...] = grad
    inner_ref[...] = grad * (1.0 - bounded_ref[...] * bounded_ref[...])


def loss_rest(own_ref, other_ref, bounded_ref, analysis_ref, before_ref, grad_ref, inner_ref,
              cross_ref, chip_ref, first_ref, second_ref, *, breadth):
    edge = before_ref.shape[1]
    analysis = analysis_ref[:, edge:]
    own = own_ref[...] - analysis
    grad = slope(own) - slope(own - (other_ref[...] - analysis))
    grad_ref[...] = grad
    inner_ref[:, :edge] = before_ref[...]
    inner_ref[:, edge:] = grad * (1.0 - bounded_ref[...] * bounded_ref[...])
    pack(inner_ref, cross_ref, chip_ref, first_ref, second_ref, breadth)


def whole_analysis(mine_ref, theirs_ref, out_ref):
    half = mine_ref.shape[1]
    first = lax.axis_index("ens") == 0
    mine, theirs = mine_ref[...], theirs_ref[...]
    out_ref[:, :half] = jnp.where(first, mine, theirs)
    out_ref[:, half:] = jnp.where(first, theirs, mine)


def crps_kernel(own1_ref, own2_ref, other1_ref, other2_ref, mine_ref, out_ref):
    half = mine_ref.shape[1]
    edge = own1_ref.shape[1]
    for part in range(2):
        @pl.when(lax.axis_index("ens") == part)
        def _():
            low, high = part * half, (part + 1) * half
            pieces = []
            if low < edge:
                pieces.append((own1_ref, other1_ref, slice(low, min(high, edge)), 0))
            if high > edge:
                start = max(low, edge)
                pieces.append((own2_ref, other2_ref, slice(start - edge, high - edge), start - low))
            for own_ref, other_ref, lanes, at in pieces:
                here = slice(at, at + lanes.stop - lanes.start)
                mine = mine_ref[:, here]
                own = own_ref[:, lanes] - mine
                other = other_ref[:, lanes] - mine
                gap = own - other
                pair = 2.0 * (soft(gap) + jnp.sqrt(jnp.full_like(gap, SMOOTH)))
                out_ref[:, here] = 0.5 * (soft(own) + soft(other)) - pair / 4.0


def loss_many(predicted, bounded, analysis):
    grouped = lax.all_to_all(predicted[None], "ens", split_axis=2, concat_axis=0, tiled=True)
    misfit = grouped - analysis[None]
    count = misfit.shape[0]

    def step(other, totals):
        differ = misfit - lax.dynamic_index_in_dim(misfit, other, 0)
        smooth_abs = jnp.sqrt(differ * differ + SMOOTH)
        return totals[0] + smooth_abs.sum(0), totals[1] + differ / smooth_abs

    sums, slopes = lax.fori_loop(
        0, count, step, (jnp.zeros_like(misfit[0]), jnp.zeros_like(misfit))
    )
    own = jnp.sqrt(misfit * misfit + SMOOTH)
    crps = jnp.mean(own, 0) - sums / (2.0 * count * (count - 1))
    grad = misfit / own - slopes / (count - 1.0)
    grad = lax.all_to_all(grad, "ens", split_axis=0, concat_axis=2, tiled=True)[0]
    return grad, grad * (1.0 - bounded * bounded), crps


def local(members, analysis, stencils, mixing):
    _, height, breadth, channels = members.shape
    bases, span = stencils.shape[:2]
    margin = span // 2
    rows = height // 2
    assert height == 2 * rows and rows + 2 * margin <= DEPTH // SLOTS and rows >= 2 * margin
    cells = height * breadth
    pair = lax.axis_size("ens") == 2
    flat = members.reshape(cells, channels)
    mine = analysis.reshape(cells, analysis.shape[2])
    rest = channels - EDGE
    packed = edges(cells, channels, breadth, margin)
    mix_flops = 6 * cells * bases * channels * channels
    stencil_flops = 6 * bases * cells * DEPTH * channels
    inner_cells, outer_cells = cells - 2 * margin * breadth, 2 * margin * breadth

    def taps(count):
        return [b16(bases, count, channels)] * 2

    def spread(cross, chip, first, second, field, band):
        cross, chip = swap_lon(cross, chip)
        first, second = swap(first, second)
        corner = f32(2 * margin * margin, channels)
        corners = call(
            functools.partial(corner_kernel, breadth=breadth, margin=margin),
            [corner, corner], [first, second], size=1 << 18, limit=4,
        )
        corners = swap_lon(*corners)
        window = b16((height + 2 * margin) * SLOTS, channels)
        xhigh, xlow, *inner = call(
            functools.partial(inner_kernel, breadth=breadth),
            [window, window] + taps(inner_cells), [field, cross, chip, band[0]],
            flops=stencil_flops * 7 // 10,
        )
        depth = pltpu.VMEM((2, DEPTH, channels), jnp.bfloat16)
        outer = call(
            functools.partial(outer_kernel, breadth=breadth), taps(outer_cells),
            [first, second, *corners, band[1], xhigh, xlow],
            scratch=[depth, depth], flops=stencil_flops * 3 // 10,
        )
        return [*inner, *outer]

    *sent, flat = call(
        functools.partial(pack_kernel, breadth=breadth), packed + [f32(cells, channels)],
        [flat], flops=10**10, size=1 << 20, limit=8,
    )
    band = bands(stencils, rows, breadth, True)
    spread0 = spread(*sent, flat, band)
    if pair:
        theirs = lax.ppermute(mine, "ens", SWAP)
    weights = call(split_mixing, [b16(*mixing.shape)] * 2, [mixing], size=mixing.size * 4)
    predicted1, bounded1 = call(
        functools.partial(forward, start=0), [f32(cells, EDGE)] * 2,
        [*spread0, *weights, flat], flops=mix_flops * EDGE // channels,
    )
    if pair:
        other1 = lax.ppermute(predicted1, "ens", SWAP)
    predicted2, bounded2 = call(
        functools.partial(forward, start=EDGE), [f32(cells, rest)] * 2,
        [*spread0, *weights, flat], flops=mix_flops * rest // channels,
    )
    back = bands(stencils, rows, breadth, False)
    if pair:
        other2 = lax.ppermute(predicted2, "ens", SWAP)
        (known,) = call(
            whole_analysis, [f32(cells, channels)], [mine, theirs],
            size=1 << 20, limit=8,
        )
        grad1, inner1 = call(
            loss_first, [f32(cells, EDGE)] * 2,
            [predicted1, other1, bounded1, known], size=1 << 20, limit=8,
        )
        grad2, inner, *sent = call(
            functools.partial(loss_rest, breadth=breadth),
            [f32(cells, rest), f32(cells, channels)] + packed,
            [predicted2, other2, bounded2, known, inner1],
            size=2 << 20, limit=8,
        )
        (crps,) = call(
            crps_kernel, [f32(*mine.shape)],
            [predicted1, predicted2, other1, other2, mine],
            size=1 << 20, limit=8,
        )
    else:
        predicted = jnp.concatenate([predicted1, predicted2], 1)
        bounded = jnp.concatenate([bounded1, bounded2], 1)
        grad, inner, crps = loss_many(predicted, bounded, mine)
        grad1, grad2 = grad[:, :EDGE], grad[:, EDGE:]
        *sent, inner = call(
            functools.partial(pack_kernel, breadth=breadth), packed + [f32(cells, channels)],
            [inner], size=1 << 20, limit=8,
        )
    (result,) = call(
        backward, [f32(cells, channels)],
        [*spread(*sent, inner, back), *weights, grad1, grad2], flops=mix_flops,
    )
    return result.reshape(members.shape), crps.reshape(analysis.shape)


def solution(mesh):
    in_specs = (P("ens", "lat", "lon", None), P("lat", "lon", "ens"), P(), P())
    out_specs = (P("ens", "lat", "lon", None), P("lat", "lon", "ens"))
    return jax.shard_map(local, mesh=mesh, in_specs=in_specs, out_specs=out_specs, check_vma=False)
```

```python
import functools

import jax
import jax.numpy as jnp
from jax import lax
from jax.experimental import pallas as pl
from jax.experimental.pallas import tpu as pltpu
from jax.sharding import PartitionSpec as P


SMOOTH = 0.01
SLOTS = 16
DEPTH = 256
CHUNKS = (2, 2)
SWAP = [(0, 1), (1, 0)]
VMEM = pl.BlockSpec(memory_space=pltpu.VMEM)


def f32(*shape):
    return jax.ShapeDtypeStruct(shape, jnp.float32)


def b16(*shape):
    return jax.ShapeDtypeStruct(shape, jnp.bfloat16)


def split(value):
    high = value.astype(jnp.bfloat16)
    low = (value - high.astype(jnp.float32)).astype(jnp.bfloat16)
    return high, low


def product(left, right, axis):
    return lax.dot_general(
        left, right, (((1,), (axis,)), ((), ())), preferred_element_type=jnp.float32
    )


def product3(left_high, left_low, right_high, right_low, axis):
    rows = left_high.shape[0]
    both = product(jnp.concatenate([left_high, left_low], 0), right_high, axis)
    return both[:rows] + both[rows:] + product(left_high, right_low, axis)


def call(body, out_shape, operands, specs=None, scratch=(), flops=0, size=0, limit=12):
    return pl.pallas_call(
        body,
        out_shape=out_shape,
        in_specs=specs or [VMEM] * len(operands),
        out_specs=[VMEM] * len(out_shape),
        scratch_shapes=scratch,
        cost_estimate=pl.CostEstimate(flops=flops, bytes_accessed=size, transcendentals=0),
        compiler_params=pltpu.CompilerParams(vmem_limit_bytes=limit << 20),
    )(*operands)


def band_kernel(stencils_ref, inner_ref, outer_ref, table_ref, in_ref, out_ref, *, rows, forward):
    bases, span, _, total = stencils_ref.shape
    blocks = inner_ref.shape[0]
    margin = span // 2
    breadth = outer_ref.shape[1] // (2 * bases * margin)
    first_row = lax.axis_index("lat") * (2 * rows)
    iota = lambda shape, axis: lax.broadcasted_iota(jnp.int32, shape, axis)

    table_ref[...] = jnp.zeros_like(table_ref)
    for base in range(bases):
        for tap in range(span):
            at = (base * 8 + tap) * 8
            table_ref[at : at + span, :total] = stencils_ref[base, tap]
    table = split(table_ref[...])

    group = blocks * SLOTS
    shifts = [margin] if forward else list(range(span))
    count = group * len(shifts)
    line, latitude = iota((count, table_ref.shape[1]), 0), iota((count, table_ref.shape[1]), 1)
    local_row = line % SLOTS
    shift = shifts[0] if forward else line // group
    wanted = first_row + (line % group) // SLOTS * rows + local_row + shift - margin
    picks = ((latitude == wanted) & (local_row < rows)).astype(jnp.float32).astype(jnp.bfloat16)

    width = table_ref.shape[0]
    tap_of = iota((group, width), 1) // 8 % 8
    stacked = []
    for part in table:
        picked = product(picks, part, 1)
        if forward:
            line = iota((group, width), 0)
            reach = first_row + line // SLOTS * rows + line % SLOTS + tap_of - margin
            taps = jnp.where((reach >= 0) & (reach < total), picked, 0.0)
        else:
            taps = jnp.zeros((group, width), jnp.float32)
            for tap in range(span):
                here = picked[tap * group : (tap + 1) * group]
                taps = jnp.where(tap_of == span - 1 - tap, here, taps)
        stacked += [taps[:, at : at + 128] for at in range(0, width, 128)]
    left = jnp.concatenate(stacked, 0).astype(jnp.bfloat16)
    pairs = width // 128

    source, target = iota((128, 256), 0), iota((128, 256), 1)
    slot = target % SLOTS
    column = jnp.where(
        slot < breadth,
        slot,
        jnp.where(slot < breadth + margin, slot - breadth - margin, slot - margin),
    )
    row_tap, column_tap = source // 8 % 8, source % 8
    to_row = target % 128 // SLOTS
    if not forward:
        row_tap, column_tap = span - 1 - row_tap, span - 1 - column_tap
    same = (row_tap == to_row) & (source // 64 == target // 128) & (slot < breadth + 2 * margin)
    same = same & (source % 8 < span) & (source // 8 % 8 < span)
    offset = jnp.where(same, column_tap - column, 1000)
    zeros = jnp.zeros((left.shape[0], 128), jnp.float32)
    for j in range(breadth):
        spread = (offset == margin - j).astype(jnp.float32).astype(jnp.bfloat16)
        both = product(left, spread, 0)
        for odd in range(2):
            wide = jnp.concatenate([both[:, odd * 128 : odd * 128 + 128], zeros], 1)
            wide = pltpu.roll(wide, 0, 1, stride=SLOTS, stride_axis=0)
            for part in range(2):
                for pair in range(pairs):
                    base = 2 * pair + odd
                    if base >= bases:
                        continue
                    for block in range(blocks):
                        at = ((part * pairs + pair) * blocks + block) * SLOTS
                        inner = margin if block == 0 else 0
                        outer = 0 if block == 0 else rows - margin
                        for ref, begin, count in (
                            (in_ref, inner, rows - margin), (out_ref, outer, margin),
                        ):
                            lines = pl.ds(base * count * breadth + j, count, stride=breadth)
                            for half in range(2):
                                ref[part, half, block, lines, :] = wide[
                                    at + begin : at + begin + count, half * 128 : half * 128 + 128
                                ]
    for source_ref, ref in ((in_ref, inner_ref), (out_ref, outer_ref)):
        for half in range(2):
            lanes = slice(half * 128, half * 128 + 128)
            both = jnp.concatenate([source_ref[0, half], source_ref[1, half]], 1)
            ref[:, :, lanes] = both.astype(jnp.bfloat16)


def bands(stencils, rows, breadth, forward):
    bases, span, _, total = stencils.shape
    margin = span // 2
    inner, outer = bases * (rows - margin) * breadth, bases * margin * breadth
    return call(
        functools.partial(band_kernel, rows=rows, forward=forward),
        [b16(2, 2 * inner, DEPTH), b16(2, 2 * outer, DEPTH)],
        [stencils],
        scratch=[
            pltpu.VMEM(((bases + 1) // 2 * 128, -(-total // 128) * 128), jnp.float32),
            pltpu.VMEM((2, DEPTH // 128, 2, inner, 128), jnp.float32),
            pltpu.VMEM((2, DEPTH // 128, 2, outer, 128), jnp.float32),
        ],
        flops=10**9, size=4 << 20,
    )


def odd_place(axis):
    return lax.axis_index(axis) % 2 == 1


def facing(tile, margin, odd):
    low, high = tile[:margin], tile[tile.shape[0] - margin :]
    return jnp.where(odd, high, low), jnp.where(odd, low, high)


def pack(field_ref, cross_ref, chip_ref, first_ref, second_ref, breadth):
    height = field_ref.shape[0] // breadth
    margin = cross_ref.shape[0] // height
    odd = odd_place("lon")
    for row in range(height):
        at = slice(row * margin, (row + 1) * margin)
        tile = field_ref[row * breadth : (row + 1) * breadth, :]
        cross_ref[at, :], chip_ref[at, :] = facing(tile, margin, odd)
    low = field_ref[: margin * breadth, :]
    high = field_ref[(height - margin) * breadth :, :]
    odd = odd_place("lat")
    first_ref[...] = jnp.where(odd, low, high)
    second_ref[...] = jnp.where(odd, high, low)


def pack_kernel(field_ref, cross_ref, chip_ref, first_ref, second_ref, kept_ref, *, breadth):
    pack(field_ref, cross_ref, chip_ref, first_ref, second_ref, breadth)
    kept_ref[...] = field_ref[...]


def edges(cells, channels, breadth, margin):
    side, row = f32(cells // breadth * margin, channels), f32(margin * breadth, channels)
    return [side, side, row, row]


def corner_kernel(first_ref, second_ref, cross_ref, chip_ref, *, breadth, margin):
    odd = odd_place("lon")
    for part, ref in enumerate((first_ref, second_ref)):
        for row in range(margin):
            at = slice((part * margin + row) * margin, (part * margin + row + 1) * margin)
            tile = ref[row * breadth : (row + 1) * breadth, :]
            cross_ref[at, :], chip_ref[at, :] = facing(tile, margin, odd)


def sides_of(cross_ref, chip_ref):
    odd = odd_place("lon")
    cross, chip = cross_ref[...], chip_ref[...]
    return jnp.where(odd, chip, cross), jnp.where(odd, cross, chip)


def widen(own, left, right):
    spare = jnp.zeros((SLOTS - own.shape[0] - left.shape[0] - right.shape[0], own.shape[1]), jnp.float32)
    return jnp.concatenate([own, left, right, spare], 0)


def inner_kernel(field_ref, cross_ref, chip_ref, band_ref, xhigh_ref, xlow_ref, shigh_ref, slow_ref, *, breadth):
    height = field_ref.shape[0] // breadth
    margin = cross_ref.shape[0] // height
    left, right = sides_of(cross_ref, chip_ref)
    bases, cells = shigh_ref.shape[:2]
    count = cells // 2
    zeros = jnp.zeros((margin * SLOTS, field_ref.shape[1]), jnp.bfloat16)
    for ref in (xhigh_ref, xlow_ref):
        ref[: margin * SLOTS, :] = zeros
        ref[(margin + height) * SLOTS :, :] = zeros
    for row in range(height):
        here = slice(row * margin, (row + 1) * margin)
        tile = widen(field_ref[row * breadth : (row + 1) * breadth, :], left[here], right[here])
        at = slice((margin + row) * SLOTS, (margin + row + 1) * SLOTS)
        xhigh_ref[at, :], xlow_ref[at, :] = split(tile)
    got = []
    for block in range(2):
        window = slice(block * (height // 2) * SLOTS, block * (height // 2) * SLOTS + DEPTH)
        got.append(banded(band_ref[block], xhigh_ref[window, :], xlow_ref[window, :]))
    keep(got, shigh_ref, slow_ref, bases, count)


def banded(band, high, low):
    lines = band.shape[0] // 2
    both = product(band, high, 0)
    return both[:lines] + both[lines:] + product(band[:lines], low, 0)


def keep(got, shigh_ref, slow_ref, bases, count):
    for base in range(bases):
        at = slice(base * count, (base + 1) * count)
        shigh_ref[base], slow_ref[base] = split(jnp.concatenate([part[at] for part in got], 0))


def outer_kernel(first_ref, second_ref, cross_ref, chip_ref, band_ref, xhigh_ref, xlow_ref,
                 shigh_ref, slow_ref, zhigh_ref, zlow_ref, *, breadth):
    margin = first_ref.shape[0] // breadth
    bases, cells = shigh_ref.shape[:2]
    edge = margin * SLOTS
    own = xhigh_ref.shape[0] - 2 * edge
    body = DEPTH - edge
    left, right = sides_of(cross_ref, chip_ref)
    odd = odd_place("lat")
    tiles = []
    for part, ref in enumerate((first_ref, second_ref)):
        rows = []
        for row in range(margin):
            here = slice((part * margin + row) * margin, (part * margin + row + 1) * margin)
            rows.append(widen(ref[row * breadth : (row + 1) * breadth, :], left[here], right[here]))
        tiles.append(jnp.concatenate(rows, 0))
    low, high = jnp.where(odd, tiles[0], tiles[1]), jnp.where(odd, tiles[1], tiles[0])
    zhigh_ref[0, :edge], zlow_ref[0, :edge] = split(low)
    zhigh_ref[1, body:], zlow_ref[1, body:] = split(high)
    for ref, source_ref in ((zhigh_ref, xhigh_ref), (zlow_ref, xlow_ref)):
        ref[0, edge:] = source_ref[edge : edge + body, :]
        ref[1, :body] = source_ref[edge + own - body : edge + own, :]
    got = [banded(band_ref[block], zhigh_ref[block], zlow_ref[block]) for block in range(2)]
    keep(got, shigh_ref, slow_ref, bases, cells // 2)


def swap_lon(cross, chip):
    count = lax.axis_size("lon")
    assert count % 2 == 0
    near = [(i, i ^ 1) for i in range(count)]
    far = [(i, (i + 1 if i % 2 else i - 1) % count) for i in range(count)]
    return lax.ppermute(cross, "lon", far), lax.ppermute(chip, "lon", near)


def swap(first, second):
    count = lax.axis_size("lat")

    def one(piece, lows):
        table = {i: i for i in range(count)}
        for low in lows:
            if low + 1 < count:
                table[low], table[low + 1] = low + 1, low
        return lax.ppermute(piece, "lat", sorted(table.items()))

    return (one(first, range(0, count, 2)), one(second, range(1, count, 2)))


def split_mixing(mixing_ref, high_ref, low_ref, *, start):
    lanes = slice(start, start + high_ref.shape[2])
    for base in range(mixing_ref.shape[0]):
        high_ref[base], low_ref[base] = split(mixing_ref[base, :, lanes])


def contract(taps, parts, axis):
    inner_high, inner_low, outer_high, outer_low = taps
    total = None
    for high_ref, low_ref, lanes in parts:
        for base in range(high_ref.shape[0]):
            high = jnp.concatenate([inner_high[base, :, lanes], outer_high[base, :, lanes]], 0)
            low = jnp.concatenate([inner_low[base, :, lanes], outer_low[base, :, lanes]], 0)
            part = product3(high, low, high_ref[base], low_ref[base], axis)
            total = part if total is None else total + part
    edge = outer_high.shape[1] // 2
    inner = inner_high.shape[1]
    return jnp.concatenate([total[inner : inner + edge], total[:inner], total[inner + edge :]], 0)


def forward(ihigh_ref, ilow_ref, ohigh_ref, olow_ref, mhigh_ref, mlow_ref, field_ref, predicted_ref, bounded_ref, *, start):
    lanes = slice(start, start + predicted_ref.shape[1])
    taps = (ihigh_ref, ilow_ref, ohigh_ref, olow_ref)
    total = contract(taps, [(mhigh_ref, mlow_ref, slice(None))], 0)
    bounded = jnp.tanh(total)
    bounded_ref[...] = bounded
    predicted_ref[...] = field_ref[:, lanes] + bounded


def backward(*refs):
    taps, rest, out_ref = refs[:4], refs[4:-1], refs[-1]
    grads, weights = rest[: len(rest) // 3], rest[len(rest) // 3 :]
    parts, start = [], 0
    for high_ref, low_ref in zip(weights[::2], weights[1::2]):
        parts.append((high_ref, low_ref, slice(start, start + high_ref.shape[2])))
        start += high_ref.shape[2]
    total = contract(taps, parts, 1)
    for grad_ref, (_, _, lanes) in zip(grads, parts):
        out_ref[:, lanes] = total[:, lanes] + grad_ref[...]


def slope(value):
    return value * lax.rsqrt(value * value + SMOOTH)


def soft(value):
    return jnp.sqrt(value * value + SMOOTH)


def loss(own_ref, other_ref, bounded_ref, analysis_ref, start):
    analysis = analysis_ref[:, start : start + own_ref.shape[1]]
    own = own_ref[...] - analysis
    grad = slope(own) - slope(own - (other_ref[...] - analysis))
    return grad, grad * (1.0 - bounded_ref[...] * bounded_ref[...])


def loss_part(own_ref, other_ref, bounded_ref, analysis_ref, grad_ref, inner_ref, *, start):
    grad_ref[...], inner_ref[...] = loss(own_ref, other_ref, bounded_ref, analysis_ref, start)


def loss_last(own_ref, other_ref, bounded_ref, analysis_ref, *rest, breadth):
    before, (grad_ref, inner_ref, cross_ref, chip_ref, first_ref, second_ref) = rest[:-6], rest[-6:]
    start = 0
    for ref in before:
        inner_ref[:, start : start + ref.shape[1]] = ref[...]
        start += ref.shape[1]
    grad_ref[...], inner_ref[:, start:] = loss(own_ref, other_ref, bounded_ref, analysis_ref, start)
    pack(inner_ref, cross_ref, chip_ref, first_ref, second_ref, breadth)


def whole_analysis(mine_ref, theirs_ref, out_ref):
    half = mine_ref.shape[1]
    first = lax.axis_index("ens") == 0
    mine, theirs = mine_ref[...], theirs_ref[...]
    out_ref[:, :half] = jnp.where(first, mine, theirs)
    out_ref[:, half:] = jnp.where(first, theirs, mine)


def crps_kernel(*refs):
    mine_ref, out_ref = refs[-2:]
    owns, others = refs[: len(refs) // 2 - 1], refs[len(refs) // 2 - 1 : -2]
    half = mine_ref.shape[1]
    for part in range(2):
        @pl.when(lax.axis_index("ens") == part)
        def _():
            low, high = part * half, (part + 1) * half
            start = 0
            for own_ref, other_ref in zip(owns, others):
                stop = start + own_ref.shape[1]
                begin, end = max(low, start), min(high, stop)
                if begin < end:
                    here = slice(begin - low, end - low)
                    lanes = slice(begin - start, end - start)
                    mine = mine_ref[:, here]
                    own = own_ref[:, lanes] - mine
                    other = other_ref[:, lanes] - mine
                    gap = own - other
                    pair = 2.0 * (soft(gap) + jnp.sqrt(jnp.full_like(gap, SMOOTH)))
                    out_ref[:, here] = 0.5 * (soft(own) + soft(other)) - pair / 4.0
                start = stop


def loss_many(predicted, bounded, analysis):
    grouped = lax.all_to_all(predicted[None], "ens", split_axis=2, concat_axis=0, tiled=True)
    misfit = grouped - analysis[None]
    count = misfit.shape[0]

    def step(other, totals):
        differ = misfit - lax.dynamic_index_in_dim(misfit, other, 0)
        smooth_abs = jnp.sqrt(differ * differ + SMOOTH)
        return totals[0] + smooth_abs.sum(0), totals[1] + differ / smooth_abs

    sums, slopes = lax.fori_loop(
        0, count, step, (jnp.zeros_like(misfit[0]), jnp.zeros_like(misfit))
    )
    own = jnp.sqrt(misfit * misfit + SMOOTH)
    crps = jnp.mean(own, 0) - sums / (2.0 * count * (count - 1))
    grad = misfit / own - slopes / (count - 1.0)
    grad = lax.all_to_all(grad, "ens", split_axis=0, concat_axis=2, tiled=True)[0]
    return grad, grad * (1.0 - bounded * bounded), crps


def local(members, analysis, stencils, mixing):
    _, height, breadth, channels = members.shape
    bases, span = stencils.shape[:2]
    margin = span // 2
    rows = height // 2
    assert height == 2 * rows and rows + 2 * margin <= DEPTH // SLOTS and rows >= 2 * margin
    cells = height * breadth
    pair = lax.axis_size("ens") == 2
    flat = members.reshape(cells, channels)
    mine = analysis.reshape(cells, analysis.shape[2])
    widths = [128 * n for n in CHUNKS]
    widths.append(channels - sum(widths))
    starts = [sum(widths[:n]) for n in range(len(widths))]
    assert widths[-1] > 0
    packed = edges(cells, channels, breadth, margin)
    mix_flops = 6 * cells * bases * channels * channels
    stencil_flops = 6 * bases * cells * DEPTH * channels
    inner_cells, outer_cells = cells - 2 * margin * breadth, 2 * margin * breadth

    def taps(count):
        return [b16(bases, count, channels)] * 2

    def spread(cross, chip, first, second, field, band):
        cross, chip = swap_lon(cross, chip)
        first, second = swap(first, second)
        corner = f32(2 * margin * margin, channels)
        corners = call(
            functools.partial(corner_kernel, breadth=breadth, margin=margin),
            [corner, corner], [first, second], size=1 << 18, limit=4,
        )
        corners = swap_lon(*corners)
        window = b16((height + 2 * margin) * SLOTS, channels)
        xhigh, xlow, *inner = call(
            functools.partial(inner_kernel, breadth=breadth),
            [window, window] + taps(inner_cells), [field, cross, chip, band[0]],
            flops=stencil_flops * 7 // 10,
        )
        depth = pltpu.VMEM((2, DEPTH, channels), jnp.bfloat16)
        outer = call(
            functools.partial(outer_kernel, breadth=breadth), taps(outer_cells),
            [first, second, *corners, band[1], xhigh, xlow],
            scratch=[depth, depth], flops=stencil_flops * 3 // 10,
        )
        return [*inner, *outer]

    *sent, flat = call(
        functools.partial(pack_kernel, breadth=breadth), packed + [f32(cells, channels)],
        [flat], flops=10**10, size=1 << 20, limit=8,
    )
    band = bands(stencils, rows, breadth, True)
    spread0 = spread(*sent, flat, band)
    if pair:
        theirs = lax.ppermute(mine, "ens", SWAP)
    weights, predicted, bounded, others = [], [], [], []
    for start, width in zip(starts, widths):
        weights += call(
            functools.partial(split_mixing, start=start),
            [b16(bases, channels, width)] * 2, [mixing], size=bases * channels * width * 4,
        )
        ahead, tanh = call(
            functools.partial(forward, start=start), [f32(cells, width)] * 2,
            [*spread0, *weights[-2:], flat], flops=mix_flops * width // channels,
        )
        predicted.append(ahead)
        bounded.append(tanh)
        if pair:
            others.append(lax.ppermute(ahead, "ens", SWAP))
    back = bands(stencils, rows, breadth, False)
    if pair:
        (known,) = call(
            whole_analysis, [f32(cells, channels)], [mine, theirs],
            size=1 << 20, limit=8,
        )
        grads, inners = [], []
        for n, (start, width) in enumerate(zip(starts, widths)):
            pieces = [predicted[n], others[n], bounded[n], known]
            if n < len(widths) - 1:
                grad, inner = call(
                    functools.partial(loss_part, start=start),
                    [f32(cells, width)] * 2, pieces, size=1 << 20, limit=8,
                )
                inners.append(inner)
            else:
                grad, inner, *sent = call(
                    functools.partial(loss_last, breadth=breadth),
                    [f32(cells, width), f32(cells, channels)] + packed, pieces + inners,
                    size=2 << 20, limit=8,
                )
            grads.append(grad)
        (crps,) = call(
            crps_kernel, [f32(*mine.shape)], [*predicted, *others, mine],
            size=1 << 20, limit=8,
        )
    else:
        grad, inner, crps = loss_many(
            jnp.concatenate(predicted, 1), jnp.concatenate(bounded, 1), mine
        )
        grads = [grad[:, start : start + width] for start, width in zip(starts, widths)]
        *sent, inner = call(
            functools.partial(pack_kernel, breadth=breadth), packed + [f32(cells, channels)],
            [inner], size=1 << 20, limit=8,
        )
    (result,) = call(
        backward, [f32(cells, channels)],
        [*spread(*sent, inner, back), *grads, *weights], flops=mix_flops,
    )
    return result.reshape(members.shape), crps.reshape(analysis.shape)


def solution(mesh):
    in_specs = (P("ens", "lat", "lon", None), P("lat", "lon", "ens"), P(), P())
    out_specs = (P("ens", "lat", "lon", None), P("lat", "lon", "ens"))
    return jax.shard_map(local, mesh=mesh, in_specs=in_specs, out_specs=out_specs, check_vma=False)
```

```python
import functools

import jax
import jax.numpy as jnp
from jax import lax
from jax.experimental import pallas as pl
from jax.experimental.pallas import tpu as pltpu
from jax.sharding import PartitionSpec as P


SMOOTH = 0.01
SLOTS = 16
DEPTH = 256
CHUNKS = (2, 2)
SWAP = [(0, 1), (1, 0)]
VMEM = pl.BlockSpec(memory_space=pltpu.VMEM)


def f32(*shape):
    return jax.ShapeDtypeStruct(shape, jnp.float32)


def b16(*shape):
    return jax.ShapeDtypeStruct(shape, jnp.bfloat16)


def split(value):
    high = value.astype(jnp.bfloat16)
    low = (value - high.astype(jnp.float32)).astype(jnp.bfloat16)
    return high, low


def product(left, right, axis):
    return lax.dot_general(
        left, right, (((1,), (axis,)), ((), ())), preferred_element_type=jnp.float32
    )


def product3(left_high, left_low, right_high, right_low, axis):
    rows = left_high.shape[0]
    both = product(jnp.concatenate([left_high, left_low], 0), right_high, axis)
    return both[:rows] + both[rows:] + product(left_high, right_low, axis)


def call(body, out_shape, operands, specs=None, scratch=(), flops=0, size=0, limit=12):
    run = pl.pallas_call(
        body,
        out_shape=out_shape,
        in_specs=specs or [VMEM] * len(operands),
        out_specs=[VMEM] * len(out_shape),
        scratch_shapes=scratch,
        cost_estimate=pl.CostEstimate(flops=flops, bytes_accessed=size, transcendentals=0),
        compiler_params=pltpu.CompilerParams(vmem_limit_bytes=limit << 20),
    )
    return run(*operands)


def band_kernel(stencils_ref, inner_ref, outer_ref, table_ref, in_ref, out_ref, *, rows, forward):
    bases, span, _, total = stencils_ref.shape
    blocks = inner_ref.shape[0]
    margin = span // 2
    breadth = outer_ref.shape[1] // (2 * bases * margin)
    first_row = lax.axis_index("lat") * (2 * rows)
    iota = lambda shape, axis: lax.broadcasted_iota(jnp.int32, shape, axis)

    table_ref[...] = jnp.zeros_like(table_ref)
    for base in range(bases):
        for tap in range(span):
            at = (base * 8 + tap) * 8
            table_ref[at : at + span, :total] = stencils_ref[base, tap]
    table = split(table_ref[...])

    group = blocks * SLOTS
    shifts = [margin] if forward else list(range(span))
    count = group * len(shifts)
    line, latitude = iota((count, table_ref.shape[1]), 0), iota((count, table_ref.shape[1]), 1)
    local_row = line % SLOTS
    shift = shifts[0] if forward else line // group
    wanted = first_row + (line % group) // SLOTS * rows + local_row + shift - margin
    picks = ((latitude == wanted) & (local_row < rows)).astype(jnp.float32).astype(jnp.bfloat16)

    width = table_ref.shape[0]
    tap_of = iota((group, width), 1) // 8 % 8
    stacked = []
    for part in table:
        picked = product(picks, part, 1)
        if forward:
            line = iota((group, width), 0)
            reach = first_row + line // SLOTS * rows + line % SLOTS + tap_of - margin
            taps = jnp.where((reach >= 0) & (reach < total), picked, 0.0)
        else:
            taps = jnp.zeros((group, width), jnp.float32)
            for tap in range(span):
                here = picked[tap * group : (tap + 1) * group]
                taps = jnp.where(tap_of == span - 1 - tap, here, taps)
        stacked += [taps[:, at : at + 128] for at in range(0, width, 128)]
    left = jnp.concatenate(stacked, 0).astype(jnp.bfloat16)
    pairs = width // 128

    source, target = iota((128, 256), 0), iota((128, 256), 1)
    slot = target % SLOTS
    column = jnp.where(
        slot < breadth,
        slot,
        jnp.where(slot < breadth + margin, slot - breadth - margin, slot - margin),
    )
    row_tap, column_tap = source // 8 % 8, source % 8
    to_row = target % 128 // SLOTS
    if not forward:
        row_tap, column_tap = span - 1 - row_tap, span - 1 - column_tap
    same = (row_tap == to_row) & (source // 64 == target // 128) & (slot < breadth + 2 * margin)
    same = same & (source % 8 < span) & (source // 8 % 8 < span)
    offset = jnp.where(same, column_tap - column, 1000)
    zeros = jnp.zeros((left.shape[0], 128), jnp.float32)
    for j in range(breadth):
        spread = (offset == margin - j).astype(jnp.float32).astype(jnp.bfloat16)
        both = product(left, spread, 0)
        for odd in range(2):
            wide = jnp.concatenate([both[:, odd * 128 : odd * 128 + 128], zeros], 1)
            wide = pltpu.roll(wide, 0, 1, stride=SLOTS, stride_axis=0)
            for part in range(2):
                for pair in range(pairs):
                    base = 2 * pair + odd
                    if base >= bases:
                        continue
                    for block in range(blocks):
                        at = ((part * pairs + pair) * blocks + block) * SLOTS
                        inner = margin if block == 0 else 0
                        outer = 0 if block == 0 else rows - margin
                        for ref, begin, count in (
                            (in_ref, inner, rows - margin), (out_ref, outer, margin),
                        ):
                            lines = pl.ds(base * count * breadth + j, count, stride=breadth)
                            for half in range(2):
                                ref[part, half, block, lines, :] = wide[
                                    at + begin : at + begin + count, half * 128 : half * 128 + 128
                                ]
    for source_ref, ref in ((in_ref, inner_ref), (out_ref, outer_ref)):
        for half in range(2):
            lanes = slice(half * 128, half * 128 + 128)
            both = jnp.concatenate([source_ref[0, half], source_ref[1, half]], 1)
            ref[:, :, lanes] = both.astype(jnp.bfloat16)


def bands(stencils, rows, breadth, forward):
    bases, span, _, total = stencils.shape
    margin = span // 2
    inner, outer = bases * (rows - margin) * breadth, bases * margin * breadth
    return call(
        functools.partial(band_kernel, rows=rows, forward=forward),
        [b16(2, 2 * inner, DEPTH), b16(2, 2 * outer, DEPTH)],
        [stencils],
        scratch=[
            pltpu.VMEM(((bases + 1) // 2 * 128, -(-total // 128) * 128), jnp.float32),
            pltpu.VMEM((2, DEPTH // 128, 2, inner, 128), jnp.float32),
            pltpu.VMEM((2, DEPTH // 128, 2, outer, 128), jnp.float32),
        ],
        flops=10**9, size=4 << 20,
    )


def odd_place(axis):
    return lax.axis_index(axis) % 2 == 1


def facing(tile, margin, odd):
    low, high = tile[:margin], tile[tile.shape[0] - margin :]
    return jnp.where(odd, high, low), jnp.where(odd, low, high)


def pack(field_ref, cross_ref, chip_ref, first_ref, second_ref, breadth):
    height = field_ref.shape[0] // breadth
    margin = cross_ref.shape[0] // height
    odd = odd_place("lon")
    for row in range(height):
        at = slice(row * margin, (row + 1) * margin)
        tile = field_ref[row * breadth : (row + 1) * breadth, :]
        cross_ref[at, :], chip_ref[at, :] = facing(tile, margin, odd)
    low = field_ref[: margin * breadth, :]
    high = field_ref[(height - margin) * breadth :, :]
    odd = odd_place("lat")
    first_ref[...] = jnp.where(odd, low, high)
    second_ref[...] = jnp.where(odd, high, low)


def pack_kernel(field_ref, cross_ref, chip_ref, first_ref, second_ref, kept_ref, *, breadth):
    pack(field_ref, cross_ref, chip_ref, first_ref, second_ref, breadth)
    kept_ref[...] = field_ref[...]


def edges(cells, channels, breadth, margin):
    side, row = f32(cells // breadth * margin, channels), f32(margin * breadth, channels)
    return [side, side, row, row]


def corner_kernel(first_ref, second_ref, cross_ref, chip_ref, *, breadth, margin):
    odd = odd_place("lon")
    count = 2 * margin * margin
    for part, ref in enumerate((first_ref, second_ref)):
        for row in range(margin):
            at = slice((part * margin + row) * margin, (part * margin + row + 1) * margin)
            tile = ref[row * breadth : (row + 1) * breadth, :]
            for target_ref, value in zip((cross_ref, chip_ref), facing(tile, margin, odd)):
                for lane in range(value.shape[1] // 128):
                    here = slice(lane * count + at.start, lane * count + at.stop)
                    target_ref[here, :] = value[:, lane * 128 : lane * 128 + 128]


def unstacked(ref, lanes):
    count = ref.shape[0] // lanes
    return jnp.concatenate([ref[n * count : (n + 1) * count, :] for n in range(lanes)], 1)


def sides_of(cross, chip):
    odd = odd_place("lon")
    return jnp.where(odd, chip, cross), jnp.where(odd, cross, chip)


def widen(own, left, right):
    spare = jnp.zeros((SLOTS - own.shape[0] - left.shape[0] - right.shape[0], own.shape[1]), jnp.float32)
    return jnp.concatenate([own, left, right, spare], 0)


def inner_kernel(field_ref, cross_ref, chip_ref, band_ref, xhigh_ref, xlow_ref, shigh_ref, slow_ref, *, breadth):
    height = field_ref.shape[0] // breadth
    margin = cross_ref.shape[0] // height
    left, right = sides_of(cross_ref[...], chip_ref[...])
    bases, cells = shigh_ref.shape[:2]
    count = cells // 2
    zeros = jnp.zeros((margin * SLOTS, field_ref.shape[1]), jnp.bfloat16)
    for ref in (xhigh_ref, xlow_ref):
        ref[: margin * SLOTS, :] = zeros
        ref[(margin + height) * SLOTS :, :] = zeros
    for row in range(height):
        here = slice(row * margin, (row + 1) * margin)
        tile = widen(field_ref[row * breadth : (row + 1) * breadth, :], left[here], right[here])
        at = slice((margin + row) * SLOTS, (margin + row + 1) * SLOTS)
        xhigh_ref[at, :], xlow_ref[at, :] = split(tile)
    got = []
    for block in range(2):
        window = slice(block * (height // 2) * SLOTS, block * (height // 2) * SLOTS + DEPTH)
        got.append(banded(band_ref[block], xhigh_ref[window, :], xlow_ref[window, :]))
    keep(got, shigh_ref, slow_ref, bases, count)


def banded(band, high, low):
    lines = band.shape[0] // 2
    both = product(band, high, 0)
    return both[:lines] + both[lines:] + product(band[:lines], low, 0)


def keep(got, shigh_ref, slow_ref, bases, count):
    for base in range(bases):
        at = slice(base * count, (base + 1) * count)
        shigh_ref[base], slow_ref[base] = split(jnp.concatenate([part[at] for part in got], 0))


def outer_kernel(first_ref, second_ref, cross_ref, chip_ref, band_ref, xhigh_ref, xlow_ref,
                 shigh_ref, slow_ref, zhigh_ref, zlow_ref, *, breadth):
    margin = first_ref.shape[0] // breadth
    bases, cells = shigh_ref.shape[:2]
    edge = margin * SLOTS
    own = xhigh_ref.shape[0] - 2 * edge
    body = DEPTH - edge
    lanes = first_ref.shape[1] // 128
    left, right = sides_of(unstacked(cross_ref, lanes), unstacked(chip_ref, lanes))
    odd = odd_place("lat")
    tiles = []
    for part, ref in enumerate((first_ref, second_ref)):
        rows = []
        for row in range(margin):
            here = slice((part * margin + row) * margin, (part * margin + row + 1) * margin)
            rows.append(widen(ref[row * breadth : (row + 1) * breadth, :], left[here], right[here]))
        tiles.append(jnp.concatenate(rows, 0))
    low, high = jnp.where(odd, tiles[0], tiles[1]), jnp.where(odd, tiles[1], tiles[0])
    zhigh_ref[0, :edge], zlow_ref[0, :edge] = split(low)
    zhigh_ref[1, body:], zlow_ref[1, body:] = split(high)
    for ref, source_ref in ((zhigh_ref, xhigh_ref), (zlow_ref, xlow_ref)):
        ref[0, edge:] = source_ref[edge : edge + body, :]
        ref[1, :body] = source_ref[edge + own - body : edge + own, :]
    got = [banded(band_ref[block], zhigh_ref[block], zlow_ref[block]) for block in range(2)]
    keep(got, shigh_ref, slow_ref, bases, cells // 2)


def swap_lon(cross, chip):
    count = lax.axis_size("lon")
    assert count % 2 == 0
    near = [(i, i ^ 1) for i in range(count)]
    far = [(i, (i + 1 if i % 2 else i - 1) % count) for i in range(count)]
    return lax.ppermute(cross, "lon", far), lax.ppermute(chip, "lon", near)


def swap(first, second):
    count = lax.axis_size("lat")

    def one(piece, lows):
        table = {i: i for i in range(count)}
        for low in lows:
            if low + 1 < count:
                table[low], table[low + 1] = low + 1, low
        return lax.ppermute(piece, "lat", sorted(table.items()))

    return (one(first, range(0, count, 2)), one(second, range(1, count, 2)))


def split_mixing(mixing_ref, high_ref, low_ref, *, start):
    lanes = slice(start, start + high_ref.shape[2])
    for base in range(mixing_ref.shape[0]):
        high_ref[base], low_ref[base] = split(mixing_ref[base, :, lanes])


def contract(taps, parts, axis):
    inner_high, inner_low, outer_high, outer_low = taps
    total = None
    for high_ref, low_ref, lanes in parts:
        for base in range(high_ref.shape[0]):
            high = jnp.concatenate([inner_high[base, :, lanes], outer_high[base, :, lanes]], 0)
            low = jnp.concatenate([inner_low[base, :, lanes], outer_low[base, :, lanes]], 0)
            part = product3(high, low, high_ref[base], low_ref[base], axis)
            total = part if total is None else total + part
    edge = outer_high.shape[1] // 2
    inner = inner_high.shape[1]
    return jnp.concatenate([total[inner : inner + edge], total[:inner], total[inner + edge :]], 0)


def forward(ihigh_ref, ilow_ref, ohigh_ref, olow_ref, mhigh_ref, mlow_ref, field_ref, predicted_ref, bounded_ref, *, start):
    lanes = slice(start, start + predicted_ref.shape[1])
    taps = (ihigh_ref, ilow_ref, ohigh_ref, olow_ref)
    total = contract(taps, [(mhigh_ref, mlow_ref, slice(None))], 0)
    bounded = jnp.tanh(total)
    bounded_ref[...] = bounded
    predicted_ref[...] = field_ref[:, lanes] + bounded


def backward(*refs):
    taps, rest, out_ref = refs[:4], refs[4:-1], refs[-1]
    grads, weights = rest[: len(rest) // 3], rest[len(rest) // 3 :]
    parts, start = [], 0
    for high_ref, low_ref in zip(weights[::2], weights[1::2]):
        parts.append((high_ref, low_ref, slice(start, start + high_ref.shape[2])))
        start += high_ref.shape[2]
    total = contract(taps, parts, 1)
    for grad_ref, (_, _, lanes) in zip(grads, parts):
        out_ref[:, lanes] = total[:, lanes] + grad_ref[...]


def slope(value):
    return value * lax.rsqrt(value * value + SMOOTH)


def soft(value):
    return jnp.sqrt(value * value + SMOOTH)


def loss(own_ref, other_ref, bounded_ref, analysis_ref, start):
    analysis = analysis_ref[:, start : start + own_ref.shape[1]]
    own = own_ref[...] - analysis
    grad = slope(own) - slope(own - (other_ref[...] - analysis))
    return grad, grad * (1.0 - bounded_ref[...] * bounded_ref[...])


def loss_part(own_ref, other_ref, bounded_ref, analysis_ref, grad_ref, inner_ref, *, start):
    grad_ref[...], inner_ref[...] = loss(own_ref, other_ref, bounded_ref, analysis_ref, start)


def loss_last(own_ref, other_ref, bounded_ref, analysis_ref, *rest, breadth):
    before, (grad_ref, inner_ref, cross_ref, chip_ref, first_ref, second_ref) = rest[:-6], rest[-6:]
    start = 0
    for ref in before:
        inner_ref[:, start : start + ref.shape[1]] = ref[...]
        start += ref.shape[1]
    grad_ref[...], inner_ref[:, start:] = loss(own_ref, other_ref, bounded_ref, analysis_ref, start)
    pack(inner_ref, cross_ref, chip_ref, first_ref, second_ref, breadth)


def whole_analysis(mine_ref, theirs_ref, out_ref):
    half = mine_ref.shape[1]
    first = lax.axis_index("ens") == 0
    mine, theirs = mine_ref[...], theirs_ref[...]
    out_ref[:, :half] = jnp.where(first, mine, theirs)
    out_ref[:, half:] = jnp.where(first, theirs, mine)


def crps_kernel(*refs):
    mine_ref, out_ref = refs[-2:]
    owns, others = refs[: len(refs) // 2 - 1], refs[len(refs) // 2 - 1 : -2]
    half = mine_ref.shape[1]
    for part in range(2):
        @pl.when(lax.axis_index("ens") == part)
        def _():
            low, high = part * half, (part + 1) * half
            start = 0
            for own_ref, other_ref in zip(owns, others):
                stop = start + own_ref.shape[1]
                begin, end = max(low, start), min(high, stop)
                if begin < end:
                    here = slice(begin - low, end - low)
                    lanes = slice(begin - start, end - start)
                    mine = mine_ref[:, here]
                    own = own_ref[:, lanes] - mine
                    other = other_ref[:, lanes] - mine
                    gap = own - other
                    pair = 2.0 * (soft(gap) + jnp.sqrt(jnp.full_like(gap, SMOOTH)))
                    out_ref[:, here] = 0.5 * (soft(own) + soft(other)) - pair / 4.0
                start = stop


def loss_many(predicted, bounded, analysis):
    grouped = lax.all_to_all(predicted[None], "ens", split_axis=2, concat_axis=0, tiled=True)
    misfit = grouped - analysis[None]
    count = misfit.shape[0]

    def step(other, totals):
        differ = misfit - lax.dynamic_index_in_dim(misfit, other, 0)
        smooth_abs = jnp.sqrt(differ * differ + SMOOTH)
        return totals[0] + smooth_abs.sum(0), totals[1] + differ / smooth_abs

    sums, slopes = lax.fori_loop(
        0, count, step, (jnp.zeros_like(misfit[0]), jnp.zeros_like(misfit))
    )
    own = jnp.sqrt(misfit * misfit + SMOOTH)
    crps = jnp.mean(own, 0) - sums / (2.0 * count * (count - 1))
    grad = misfit / own - slopes / (count - 1.0)
    grad = lax.all_to_all(grad, "ens", split_axis=0, concat_axis=2, tiled=True)[0]
    return grad, grad * (1.0 - bounded * bounded), crps


def local(members, analysis, stencils, mixing):
    _, height, breadth, channels = members.shape
    bases, span = stencils.shape[:2]
    margin = span // 2
    rows = height // 2
    assert height == 2 * rows and rows + 2 * margin <= DEPTH // SLOTS and rows >= 2 * margin
    cells = height * breadth
    pair = lax.axis_size("ens") == 2
    flat = members.reshape(cells, channels)
    mine = analysis.reshape(cells, analysis.shape[2])
    widths = [128 * n for n in CHUNKS]
    widths.append(channels - sum(widths))
    starts = [sum(widths[:n]) for n in range(len(widths))]
    assert widths[-1] > 0
    packed = edges(cells, channels, breadth, margin)
    mix_flops = 6 * cells * bases * channels * channels
    stencil_flops = 6 * bases * cells * DEPTH * channels
    inner_cells, outer_cells = cells - 2 * margin * breadth, 2 * margin * breadth

    def taps(count):
        return [b16(bases, count, channels)] * 2

    def spread(cross, chip, first, second, field, band):
        cross, chip = swap_lon(cross, chip)
        first, second = swap(first, second)
        corner = f32(channels // 128 * 2 * margin * margin, 128)
        corners = call(
            functools.partial(corner_kernel, breadth=breadth, margin=margin),
            [corner, corner], [first, second], size=1 << 18, limit=4,
        )
        corners = swap_lon(*corners)
        window = b16((height + 2 * margin) * SLOTS, channels)
        xhigh, xlow, *inner = call(
            functools.partial(inner_kernel, breadth=breadth),
            [window, window] + taps(inner_cells), [field, cross, chip, band[0]],
            flops=stencil_flops * 7 // 10,
        )
        depth = pltpu.VMEM((2, DEPTH, channels), jnp.bfloat16)
        outer = call(
            functools.partial(outer_kernel, breadth=breadth), taps(outer_cells),
            [first, second, *corners, band[1], xhigh, xlow],
            scratch=[depth, depth], flops=stencil_flops * 3 // 10,
        )
        return [*inner, *outer]

    *sent, flat = call(
        functools.partial(pack_kernel, breadth=breadth), packed + [f32(cells, channels)],
        [flat], flops=10**10, size=1 << 20, limit=8,
    )
    band = bands(stencils, rows, breadth, True)
    spread0 = spread(*sent, flat, band)
    if pair:
        theirs = lax.ppermute(mine, "ens", SWAP)
    weights, predicted, bounded, others = [], [], [], []
    for start, width in zip(starts, widths):
        weights += call(
            functools.partial(split_mixing, start=start),
            [b16(bases, channels, width)] * 2, [mixing], size=bases * channels * width * 4,
        )
        ahead, tanh = call(
            functools.partial(forward, start=start), [f32(cells, width)] * 2,
            [*spread0, *weights[-2:], flat], flops=mix_flops * width // channels,
        )
        predicted.append(ahead)
        bounded.append(tanh)
        if pair:
            others.append(lax.ppermute(ahead, "ens", SWAP))
    back = bands(stencils, rows, breadth, False)
    if pair:
        (known,) = call(
            whole_analysis, [f32(cells, channels)], [mine, theirs],
            size=1 << 20, limit=8,
        )
        grads, inners = [], []
        for n, (start, width) in enumerate(zip(starts, widths)):
            pieces = [predicted[n], others[n], bounded[n], known]
            if n < len(widths) - 1:
                grad, inner = call(
                    functools.partial(loss_part, start=start),
                    [f32(cells, width)] * 2, pieces, size=1 << 20, limit=8,
                )
                inners.append(inner)
            else:
                grad, inner, *sent = call(
                    functools.partial(loss_last, breadth=breadth),
                    [f32(cells, width), f32(cells, channels)] + packed, pieces + inners,
                    size=2 << 20, limit=8,
                )
            grads.append(grad)
        (crps,) = call(
            crps_kernel, [f32(*mine.shape)], [*predicted, *others, mine],
            size=1 << 20, limit=8,
        )
    else:
        grad, inner, crps = loss_many(
            jnp.concatenate(predicted, 1), jnp.concatenate(bounded, 1), mine
        )
        grads = [grad[:, start : start + width] for start, width in zip(starts, widths)]
        *sent, inner = call(
            functools.partial(pack_kernel, breadth=breadth), packed + [f32(cells, channels)],
            [inner], size=1 << 20, limit=8,
        )
    (result,) = call(
        backward, [f32(cells, channels)],
        [*spread(*sent, inner, back), *grads, *weights], flops=mix_flops,
    )
    return result.reshape(members.shape), crps.reshape(analysis.shape)


def solution(mesh):
    in_specs = (P("ens", "lat", "lon", None), P("lat", "lon", "ens"), P(), P())
    out_specs = (P("ens", "lat", "lon", None), P("lat", "lon", "ens"))
    return jax.shard_map(local, mesh=mesh, in_specs=in_specs, out_specs=out_specs, check_vma=False)
```

```python
import functools

import jax
import jax.numpy as jnp
from jax import lax
from jax.experimental import pallas as pl
from jax.experimental.pallas import tpu as pltpu
from jax.sharding import PartitionSpec as P


SMOOTH = 0.01
SLOTS = 16
DEPTH = 256
CHUNKS = (2, 2)
EARLY = 2
SWAP = [(0, 1), (1, 0)]
VMEM = pl.BlockSpec(memory_space=pltpu.VMEM)


def f32(*shape):
    return jax.ShapeDtypeStruct(shape, jnp.float32)


def b16(*shape):
    return jax.ShapeDtypeStruct(shape, jnp.bfloat16)


def split(value):
    high = value.astype(jnp.bfloat16)
    low = (value - high.astype(jnp.float32)).astype(jnp.bfloat16)
    return high, low


def product(left, right, axis):
    return lax.dot_general(
        left, right, (((1,), (axis,)), ((), ())), preferred_element_type=jnp.float32
    )


def product3(left_high, left_low, right_high, right_low, axis):
    rows = left_high.shape[0]
    both = product(jnp.concatenate([left_high, left_low], 0), right_high, axis)
    return both[:rows] + both[rows:] + product(left_high, right_low, axis)


def call(body, out_shape, operands, specs=None, scratch=(), flops=0, size=0, limit=12):
    run = pl.pallas_call(
        body,
        out_shape=out_shape,
        in_specs=specs or [VMEM] * len(operands),
        out_specs=[VMEM] * len(out_shape),
        scratch_shapes=scratch,
        cost_estimate=pl.CostEstimate(flops=flops, bytes_accessed=size, transcendentals=0),
        compiler_params=pltpu.CompilerParams(vmem_limit_bytes=limit << 20),
    )
    return run(*operands)


def band_kernel(stencils_ref, inner_ref, outer_ref, table_ref, in_ref, out_ref, *, rows, forward):
    bases, span, _, total = stencils_ref.shape
    blocks = inner_ref.shape[0]
    margin = span // 2
    breadth = outer_ref.shape[1] // (2 * bases * margin)
    first_row = lax.axis_index("lat") * (2 * rows)
    iota = lambda shape, axis: lax.broadcasted_iota(jnp.int32, shape, axis)

    table_ref[...] = jnp.zeros_like(table_ref)
    for base in range(bases):
        for tap in range(span):
            at = (base * 8 + tap) * 8
            table_ref[at : at + span, :total] = stencils_ref[base, tap]
    table = split(table_ref[...])

    group = blocks * SLOTS
    shifts = [margin] if forward else list(range(span))
    count = group * len(shifts)
    line, latitude = iota((count, table_ref.shape[1]), 0), iota((count, table_ref.shape[1]), 1)
    local_row = line % SLOTS
    shift = shifts[0] if forward else line // group
    wanted = first_row + (line % group) // SLOTS * rows + local_row + shift - margin
    picks = ((latitude == wanted) & (local_row < rows)).astype(jnp.float32).astype(jnp.bfloat16)

    width = table_ref.shape[0]
    tap_of = iota((group, width), 1) // 8 % 8
    stacked = []
    for part in table:
        picked = product(picks, part, 1)
        if forward:
            line = iota((group, width), 0)
            reach = first_row + line // SLOTS * rows + line % SLOTS + tap_of - margin
            taps = jnp.where((reach >= 0) & (reach < total), picked, 0.0)
        else:
            taps = jnp.zeros((group, width), jnp.float32)
            for tap in range(span):
                here = picked[tap * group : (tap + 1) * group]
                taps = jnp.where(tap_of == span - 1 - tap, here, taps)
        stacked += [taps[:, at : at + 128] for at in range(0, width, 128)]
    left = jnp.concatenate(stacked, 0).astype(jnp.bfloat16)
    pairs = width // 128

    source, target = iota((128, 256), 0), iota((128, 256), 1)
    slot = target % SLOTS
    column = jnp.where(
        slot < breadth,
        slot,
        jnp.where(slot < breadth + margin, slot - breadth - margin, slot - margin),
    )
    row_tap, column_tap = source // 8 % 8, source % 8
    to_row = target % 128 // SLOTS
    if not forward:
        row_tap, column_tap = span - 1 - row_tap, span - 1 - column_tap
    same = (row_tap == to_row) & (source // 64 == target // 128) & (slot < breadth + 2 * margin)
    same = same & (source % 8 < span) & (source // 8 % 8 < span)
    offset = jnp.where(same, column_tap - column, 1000)
    zeros = jnp.zeros((left.shape[0], 128), jnp.float32)
    for j in range(breadth):
        spread = (offset == margin - j).astype(jnp.float32).astype(jnp.bfloat16)
        both = product(left, spread, 0)
        for odd in range(2):
            wide = jnp.concatenate([both[:, odd * 128 : odd * 128 + 128], zeros], 1)
            wide = pltpu.roll(wide, 0, 1, stride=SLOTS, stride_axis=0)
            for part in range(2):
                for pair in range(pairs):
                    base = 2 * pair + odd
                    if base >= bases:
                        continue
                    for block in range(blocks):
                        at = ((part * pairs + pair) * blocks + block) * SLOTS
                        inner = margin if block == 0 else 0
                        outer = 0 if block == 0 else rows - margin
                        for ref, begin, count in (
                            (in_ref, inner, rows - margin), (out_ref, outer, margin),
                        ):
                            lines = pl.ds(base * count * breadth + j, count, stride=breadth)
                            for half in range(2):
                                ref[part, half, block, lines, :] = wide[
                                    at + begin : at + begin + count, half * 128 : half * 128 + 128
                                ]
    for source_ref, ref in ((in_ref, inner_ref), (out_ref, outer_ref)):
        for half in range(2):
            lanes = slice(half * 128, half * 128 + 128)
            both = jnp.concatenate([source_ref[0, half], source_ref[1, half]], 1)
            ref[:, :, lanes] = both.astype(jnp.bfloat16)


def bands(stencils, rows, breadth, forward):
    bases, span, _, total = stencils.shape
    margin = span // 2
    inner, outer = bases * (rows - margin) * breadth, bases * margin * breadth
    return call(
        functools.partial(band_kernel, rows=rows, forward=forward),
        [b16(2, 2 * inner, DEPTH), b16(2, 2 * outer, DEPTH)],
        [stencils],
        scratch=[
            pltpu.VMEM(((bases + 1) // 2 * 128, -(-total // 128) * 128), jnp.float32),
            pltpu.VMEM((2, DEPTH // 128, 2, inner, 128), jnp.float32),
            pltpu.VMEM((2, DEPTH // 128, 2, outer, 128), jnp.float32),
        ],
        flops=10**9, size=4 << 20,
    )


def odd_place(axis):
    return lax.axis_index(axis) % 2 == 1


def facing(tile, margin, odd):
    low, high = tile[:margin], tile[tile.shape[0] - margin :]
    return jnp.where(odd, high, low), jnp.where(odd, low, high)


def pack(field_ref, cross_ref, chip_ref, first_ref, second_ref, breadth):
    height = field_ref.shape[0] // breadth
    margin = cross_ref.shape[0] // height
    odd = odd_place("lon")
    for row in range(height):
        at = slice(row * margin, (row + 1) * margin)
        tile = field_ref[row * breadth : (row + 1) * breadth, :]
        cross_ref[at, :], chip_ref[at, :] = facing(tile, margin, odd)
    low = field_ref[: margin * breadth, :]
    high = field_ref[(height - margin) * breadth :, :]
    odd = odd_place("lat")
    first_ref[...] = jnp.where(odd, low, high)
    second_ref[...] = jnp.where(odd, high, low)


def pack_kernel(field_ref, cross_ref, chip_ref, first_ref, second_ref, kept_ref, *, breadth):
    pack(field_ref, cross_ref, chip_ref, first_ref, second_ref, breadth)
    kept_ref[...] = field_ref[...]


def edges(cells, channels, breadth, margin):
    side, row = f32(cells // breadth * margin, channels), f32(margin * breadth, channels)
    return [side, side, row, row]


def corner_kernel(first_ref, second_ref, cross_ref, chip_ref, *, breadth, margin):
    odd = odd_place("lon")
    count = 2 * margin * margin
    for part, ref in enumerate((first_ref, second_ref)):
        for row in range(margin):
            at = slice((part * margin + row) * margin, (part * margin + row + 1) * margin)
            tile = ref[row * breadth : (row + 1) * breadth, :]
            for target_ref, value in zip((cross_ref, chip_ref), facing(tile, margin, odd)):
                for lane in range(value.shape[1] // 128):
                    here = slice(lane * count + at.start, lane * count + at.stop)
                    target_ref[here, :] = value[:, lane * 128 : lane * 128 + 128]


def unstacked(ref, lanes):
    count = ref.shape[0] // lanes
    return jnp.concatenate([ref[n * count : (n + 1) * count, :] for n in range(lanes)], 1)


def sides_of(cross, chip):
    odd = odd_place("lon")
    return jnp.where(odd, chip, cross), jnp.where(odd, cross, chip)


def widen(own, left, right):
    spare = jnp.zeros((SLOTS - own.shape[0] - left.shape[0] - right.shape[0], own.shape[1]), jnp.float32)
    return jnp.concatenate([own, left, right, spare], 0)


def inner_kernel(field_ref, cross_ref, chip_ref, band_ref, xhigh_ref, xlow_ref, shigh_ref, slow_ref, *, breadth):
    height = field_ref.shape[0] // breadth
    margin = cross_ref.shape[0] // height
    left, right = sides_of(cross_ref[...], chip_ref[...])
    bases, cells = shigh_ref.shape[:2]
    count = cells // 2
    zeros = jnp.zeros((margin * SLOTS, field_ref.shape[1]), jnp.bfloat16)
    for ref in (xhigh_ref, xlow_ref):
        ref[: margin * SLOTS, :] = zeros
        ref[(margin + height) * SLOTS :, :] = zeros
    for row in range(height):
        here = slice(row * margin, (row + 1) * margin)
        tile = widen(field_ref[row * breadth : (row + 1) * breadth, :], left[here], right[here])
        at = slice((margin + row) * SLOTS, (margin + row + 1) * SLOTS)
        xhigh_ref[at, :], xlow_ref[at, :] = split(tile)
    got = []
    for block in range(2):
        window = slice(block * (height // 2) * SLOTS, block * (height // 2) * SLOTS + DEPTH)
        got.append(banded(band_ref[block], xhigh_ref[window, :], xlow_ref[window, :]))
    keep(got, shigh_ref, slow_ref, bases, count)


def banded(band, high, low):
    lines = band.shape[0] // 2
    both = product(band, high, 0)
    return both[:lines] + both[lines:] + product(band[:lines], low, 0)


def keep(got, shigh_ref, slow_ref, bases, count):
    for base in range(bases):
        at = slice(base * count, (base + 1) * count)
        shigh_ref[base], slow_ref[base] = split(jnp.concatenate([part[at] for part in got], 0))


def outer_kernel(first_ref, second_ref, cross_ref, chip_ref, band_ref, xhigh_ref, xlow_ref,
                 shigh_ref, slow_ref, zhigh_ref, zlow_ref, *, breadth):
    margin = first_ref.shape[0] // breadth
    bases, cells = shigh_ref.shape[:2]
    edge = margin * SLOTS
    own = xhigh_ref.shape[0] - 2 * edge
    body = DEPTH - edge
    lanes = first_ref.shape[1] // 128
    left, right = sides_of(unstacked(cross_ref, lanes), unstacked(chip_ref, lanes))
    odd = odd_place("lat")
    tiles = []
    for part, ref in enumerate((first_ref, second_ref)):
        rows = []
        for row in range(margin):
            here = slice((part * margin + row) * margin, (part * margin + row + 1) * margin)
            rows.append(widen(ref[row * breadth : (row + 1) * breadth, :], left[here], right[here]))
        tiles.append(jnp.concatenate(rows, 0))
    low, high = jnp.where(odd, tiles[0], tiles[1]), jnp.where(odd, tiles[1], tiles[0])
    zhigh_ref[0, :edge], zlow_ref[0, :edge] = split(low)
    zhigh_ref[1, body:], zlow_ref[1, body:] = split(high)
    for ref, source_ref in ((zhigh_ref, xhigh_ref), (zlow_ref, xlow_ref)):
        ref[0, edge:] = source_ref[edge : edge + body, :]
        ref[1, :body] = source_ref[edge + own - body : edge + own, :]
    got = [banded(band_ref[block], zhigh_ref[block], zlow_ref[block]) for block in range(2)]
    keep(got, shigh_ref, slow_ref, bases, cells // 2)


def swap_lon(cross, chip):
    count = lax.axis_size("lon")
    assert count % 2 == 0
    near = [(i, i ^ 1) for i in range(count)]
    far = [(i, (i + 1 if i % 2 else i - 1) % count) for i in range(count)]
    return lax.ppermute(cross, "lon", far), lax.ppermute(chip, "lon", near)


def swap(first, second):
    count = lax.axis_size("lat")

    def one(piece, lows):
        table = {i: i for i in range(count)}
        for low in lows:
            if low + 1 < count:
                table[low], table[low + 1] = low + 1, low
        return lax.ppermute(piece, "lat", sorted(table.items()))

    return (one(first, range(0, count, 2)), one(second, range(1, count, 2)))


def split_mixing(mixing_ref, high_ref, low_ref, *, start):
    lanes = slice(start, start + high_ref.shape[2])
    for base in range(mixing_ref.shape[0]):
        high_ref[base], low_ref[base] = split(mixing_ref[base, :, lanes])


def joined(inner_ref, outer_ref, base, lanes):
    return jnp.concatenate([inner_ref[base, :, lanes], outer_ref[base, :, lanes]], 0)


def contract(pairs, parts, axis, bases, total=None):
    high, low = pairs
    for high_ref, low_ref, lanes in parts:
        for base in bases:
            part = product3(high(base, lanes), low(base, lanes), high_ref[base], low_ref[base], axis)
            total = part if total is None else total + part
    return total


def only(ref):
    return lambda base, lanes: ref[base, :, lanes]


def both(inner_ref, outer_ref):
    return functools.partial(joined, inner_ref, outer_ref)


def ordered(total, outer):
    edge = outer // 2
    inner = total.shape[0] - outer
    return jnp.concatenate([total[inner : inner + edge], total[:inner], total[inner + edge :]], 0)


def forward(ihigh_ref, ilow_ref, ohigh_ref, olow_ref, mhigh_ref, mlow_ref, field_ref, predicted_ref, bounded_ref, *, start):
    lanes = slice(start, start + predicted_ref.shape[1])
    pairs = both(ihigh_ref, ohigh_ref), both(ilow_ref, olow_ref)
    bases = range(mhigh_ref.shape[0])
    total = contract(pairs, [(mhigh_ref, mlow_ref, slice(None))], 0, bases)
    total = ordered(total, ohigh_ref.shape[1])
    bounded = jnp.tanh(total)
    bounded_ref[...] = bounded
    predicted_ref[...] = field_ref[:, lanes] + bounded


def spans(weights):
    parts, start = [], 0
    for high_ref, low_ref in zip(weights[::2], weights[1::2]):
        parts.append((high_ref, low_ref, slice(start, start + high_ref.shape[2])))
        start += high_ref.shape[2]
    return parts


def adjoint_early(ihigh_ref, ilow_ref, *refs):
    weights, out_ref = refs[:-1], refs[-1]
    out_ref[...] = contract((only(ihigh_ref), only(ilow_ref)), spans(weights), 1, range(EARLY))


def backward(early_ref, ihigh_ref, ilow_ref, ohigh_ref, olow_ref, *refs):
    rest, out_ref = refs[:-1], refs[-1]
    grads, weights = rest[: len(rest) // 3], rest[len(rest) // 3 :]
    parts = spans(weights)
    outer = contract((only(ohigh_ref), only(olow_ref)), parts, 1, range(EARLY))
    pairs = both(ihigh_ref, ohigh_ref), both(ilow_ref, olow_ref)
    total = contract(pairs, parts, 1, range(EARLY, ihigh_ref.shape[0]))
    total = total + jnp.concatenate([early_ref[...], outer], 0)
    total = ordered(total, ohigh_ref.shape[1])
    for grad_ref, (_, _, lanes) in zip(grads, parts):
        out_ref[:, lanes] = total[:, lanes] + grad_ref[...]


def slope(value):
    return value * lax.rsqrt(value * value + SMOOTH)


def soft(value):
    return jnp.sqrt(value * value + SMOOTH)


def loss(own_ref, other_ref, bounded_ref, analysis_ref, start):
    analysis = analysis_ref[:, start : start + own_ref.shape[1]]
    own = own_ref[...] - analysis
    grad = slope(own) - slope(own - (other_ref[...] - analysis))
    return grad, grad * (1.0 - bounded_ref[...] * bounded_ref[...])


def loss_part(own_ref, other_ref, bounded_ref, analysis_ref, grad_ref, inner_ref, *, start):
    grad_ref[...], inner_ref[...] = loss(own_ref, other_ref, bounded_ref, analysis_ref, start)


def loss_last(own_ref, other_ref, bounded_ref, analysis_ref, *rest, breadth):
    before, (grad_ref, inner_ref, cross_ref, chip_ref, first_ref, second_ref) = rest[:-6], rest[-6:]
    start = 0
    for ref in before:
        inner_ref[:, start : start + ref.shape[1]] = ref[...]
        start += ref.shape[1]
    grad_ref[...], inner_ref[:, start:] = loss(own_ref, other_ref, bounded_ref, analysis_ref, start)
    pack(inner_ref, cross_ref, chip_ref, first_ref, second_ref, breadth)


def whole_analysis(mine_ref, theirs_ref, out_ref):
    half = mine_ref.shape[1]
    first = lax.axis_index("ens") == 0
    mine, theirs = mine_ref[...], theirs_ref[...]
    out_ref[:, :half] = jnp.where(first, mine, theirs)
    out_ref[:, half:] = jnp.where(first, theirs, mine)


def crps_kernel(*refs):
    mine_ref, out_ref = refs[-2:]
    owns, others = refs[: len(refs) // 2 - 1], refs[len(refs) // 2 - 1 : -2]
    half = mine_ref.shape[1]
    for part in range(2):
        @pl.when(lax.axis_index("ens") == part)
        def _():
            low, high = part * half, (part + 1) * half
            start = 0
            for own_ref, other_ref in zip(owns, others):
                stop = start + own_ref.shape[1]
                begin, end = max(low, start), min(high, stop)
                if begin < end:
                    here = slice(begin - low, end - low)
                    lanes = slice(begin - start, end - start)
                    mine = mine_ref[:, here]
                    own = own_ref[:, lanes] - mine
                    other = other_ref[:, lanes] - mine
                    gap = own - other
                    pair = 2.0 * (soft(gap) + jnp.sqrt(jnp.full_like(gap, SMOOTH)))
                    out_ref[:, here] = 0.5 * (soft(own) + soft(other)) - pair / 4.0
                start = stop


def loss_many(predicted, bounded, analysis):
    grouped = lax.all_to_all(predicted[None], "ens", split_axis=2, concat_axis=0, tiled=True)
    misfit = grouped - analysis[None]
    count = misfit.shape[0]

    def step(other, totals):
        differ = misfit - lax.dynamic_index_in_dim(misfit, other, 0)
        smooth_abs = jnp.sqrt(differ * differ + SMOOTH)
        return totals[0] + smooth_abs.sum(0), totals[1] + differ / smooth_abs

    sums, slopes = lax.fori_loop(
        0, count, step, (jnp.zeros_like(misfit[0]), jnp.zeros_like(misfit))
    )
    own = jnp.sqrt(misfit * misfit + SMOOTH)
    crps = jnp.mean(own, 0) - sums / (2.0 * count * (count - 1))
    grad = misfit / own - slopes / (count - 1.0)
    grad = lax.all_to_all(grad, "ens", split_axis=0, concat_axis=2, tiled=True)[0]
    return grad, grad * (1.0 - bounded * bounded), crps


def local(members, analysis, stencils, mixing):
    _, height, breadth, channels = members.shape
    bases, span = stencils.shape[:2]
    margin = span // 2
    rows = height // 2
    assert height == 2 * rows and rows + 2 * margin <= DEPTH // SLOTS and rows >= 2 * margin
    cells = height * breadth
    pair = lax.axis_size("ens") == 2
    flat = members.reshape(cells, channels)
    mine = analysis.reshape(cells, analysis.shape[2])
    widths = [128 * n for n in CHUNKS]
    widths.append(channels - sum(widths))
    starts = [sum(widths[:n]) for n in range(len(widths))]
    assert widths[-1] > 0
    packed = edges(cells, channels, breadth, margin)
    mix_flops = 6 * cells * bases * channels * channels
    stencil_flops = 6 * bases * cells * DEPTH * channels
    inner_cells, outer_cells = cells - 2 * margin * breadth, 2 * margin * breadth

    def taps(count):
        return [b16(bases, count, channels)] * 2

    def spread(cross, chip, first, second, field, band):
        cross, chip = swap_lon(cross, chip)
        first, second = swap(first, second)
        corner = f32(channels // 128 * 2 * margin * margin, 128)
        corners = call(
            functools.partial(corner_kernel, breadth=breadth, margin=margin),
            [corner, corner], [first, second], size=1 << 18, limit=4,
        )
        corners = swap_lon(*corners)
        window = b16((height + 2 * margin) * SLOTS, channels)
        xhigh, xlow, *inner = call(
            functools.partial(inner_kernel, breadth=breadth),
            [window, window] + taps(inner_cells), [field, cross, chip, band[0]],
            flops=stencil_flops * 7 // 10,
        )
        depth = pltpu.VMEM((2, DEPTH, channels), jnp.bfloat16)
        outer = call(
            functools.partial(outer_kernel, breadth=breadth), taps(outer_cells),
            [first, second, *corners, band[1], xhigh, xlow],
            scratch=[depth, depth], flops=stencil_flops * 3 // 10,
        )
        return inner, outer

    *sent, flat = call(
        functools.partial(pack_kernel, breadth=breadth), packed + [f32(cells, channels)],
        [flat], flops=10**10, size=1 << 20, limit=8,
    )
    band = bands(stencils, rows, breadth, True)
    inner0, outer0 = spread(*sent, flat, band)
    if pair:
        theirs = lax.ppermute(mine, "ens", SWAP)
    weights, predicted, bounded, others = [], [], [], []
    for start, width in zip(starts, widths):
        weights += call(
            functools.partial(split_mixing, start=start),
            [b16(bases, channels, width)] * 2, [mixing], size=bases * channels * width * 4,
        )
        ahead, tanh = call(
            functools.partial(forward, start=start), [f32(cells, width)] * 2,
            [*inner0, *outer0, *weights[-2:], flat], flops=mix_flops * width // channels,
        )
        predicted.append(ahead)
        bounded.append(tanh)
        if pair:
            others.append(lax.ppermute(ahead, "ens", SWAP))
    back = bands(stencils, rows, breadth, False)
    if pair:
        (known,) = call(
            whole_analysis, [f32(cells, channels)], [mine, theirs],
            size=1 << 20, limit=8,
        )
        grads, inners = [], []
        for n, (start, width) in enumerate(zip(starts, widths)):
            pieces = [predicted[n], others[n], bounded[n], known]
            if n < len(widths) - 1:
                grad, inner = call(
                    functools.partial(loss_part, start=start),
                    [f32(cells, width)] * 2, pieces, size=1 << 20, limit=8,
                )
                inners.append(inner)
            else:
                grad, inner, *sent = call(
                    functools.partial(loss_last, breadth=breadth),
                    [f32(cells, width), f32(cells, channels)] + packed, pieces + inners,
                    size=2 << 20, limit=8,
                )
            grads.append(grad)
        (crps,) = call(
            crps_kernel, [f32(*mine.shape)], [*predicted, *others, mine],
            size=1 << 20, limit=8,
        )
    else:
        grad, inner, crps = loss_many(
            jnp.concatenate(predicted, 1), jnp.concatenate(bounded, 1), mine
        )
        grads = [grad[:, start : start + width] for start, width in zip(starts, widths)]
        *sent, inner = call(
            functools.partial(pack_kernel, breadth=breadth), packed + [f32(cells, channels)],
            [inner], size=1 << 20, limit=8,
        )
    inner1, outer1 = spread(*sent, inner, back)
    (early,) = call(
        adjoint_early, [f32(inner_cells, channels)], [*inner1, *weights],
        flops=mix_flops * EARLY // bases,
    )
    (result,) = call(
        backward, [f32(cells, channels)],
        [early, *inner1, *outer1, *grads, *weights], flops=mix_flops,
    )
    return result.reshape(members.shape), crps.reshape(analysis.shape)


def solution(mesh):
    in_specs = (P("ens", "lat", "lon", None), P("lat", "lon", "ens"), P(), P())
    out_specs = (P("ens", "lat", "lon", None), P("lat", "lon", "ens"))
    return jax.shard_map(local, mesh=mesh, in_specs=in_specs, out_specs=out_specs, check_vma=False)
```
